256 devices in a mesh: dom: 64 (over z, x_lo, y), dir: 4 (over x_hi, core).
Axes of the slice: x: 4 (x_hi: 2, x_lo: 2; x = x_hi * 2 + x_lo), y: 4, z: 8, core: 2. Of those that a mesh axis runs over, the one named last changes fastest.
Arguments:
- action: float32 [64, 32, 32768], P('dir', None, 'dom'), may hold values from -6 to 6
- edge_angle: float32 [6, 32768], P(None, 'dom'), may hold values from -3.140625 to 3.140625
- edge_speed: float32 [6, 32768], P(None, 'dom'), may hold values from 0.3 to 3
- neighbours: int32 [6, 32768], P(None, 'dom'), may hold values from 0 to 575, as said below
- send_rows: int32 [2, 2048], P(None, 'dom'), may hold values from 0 to 511, as said below
- refract_rate: float32 [32, 32768], P(None, 'dom'), may hold values from -0.45 to 0.45
- refract_angle: float32 [32768], P('dom'), may hold values from -3.140625 to 3.140625
- shift_rate: float32 [32, 32768], P(None, 'dom'), may hold values from -0.45 to 0.45
Outputs:
- wave_action: float32 [64, 32, 32768], P('dir', None, 'dom')
The draws below stay inside these ranges and needn't reach their ends.
Inputs may be any that keep to these rules, and one draw needn't show every extreme that they name: `neighbours`: slots below 512 are the partition's own nodes, then 32 slots from the lower and 32 from the upper neighbouring partition. `send_rows`: local node numbers within the sending partition.
All inputs are finite; a program needn't handle non-finite values.
Results may differ from the reference program's by a relative error of at most 0.00002.
Values sent between devices are 32-bit elements; how exact they have to be, the bound alone decides.
No kernel may reach another device: no remote copies, remote signals or barrier semaphores. Data moves between devices by JAX's collectives and lax.ppermute only.
A program may use at most 64 MiB of HBM per device.

```python
import math
import jax
import jax.numpy as jnp
from jax import lax

NDIR = 64
NFREQ = 32
NEIGH = 6
SWEEPS = 3
NODE_DEV = 512
GHOST = 32
NODES = 32768
N_DOM = 64


def draw_neighbours(key, part):
    keys = jax.random.split(jax.random.fold_in(key, 5), 3)
    local_slots = jax.random.randint(keys[0], (NEIGH, NODES), 0, NODE_DEV, dtype=jnp.int32)
    shared_slots = jax.random.randint(keys[1], (NEIGH, NODES), NODE_DEV, NODE_DEV + 2 * GHOST, dtype=jnp.int32)
    chooser = jax.random.randint(keys[2], (NEIGH, NODES), 0, 100, dtype=jnp.int32)
    values = jnp.where(chooser < 6, shared_slots, local_slots)
    local = jnp.arange(NODES, dtype=jnp.int32) % NODE_DEV
    last_row = (jnp.arange(NEIGH, dtype=jnp.int32) == NEIGH - 1)[:, None]
    values = jnp.where(jnp.logical_and(last_row, (local == 0)[None, :]), NODE_DEV + 2 * GHOST - 1, values)
    values = jnp.where(jnp.logical_and(last_row, (local == 1)[None, :]), 0, values)
    values = jnp.where(jnp.logical_and(last_row, (local == 2)[None, :]), NODE_DEV, values)
    return values.astype(jnp.int32)


def draw_send_rows(key, part):
    parts_count = NODES // NODE_DEV
    keys = jax.random.split(jax.random.fold_in(key, 11), 2 * parts_count)

    def one_list(subkey):
        middle = jax.random.permutation(subkey, jnp.arange(1, NODE_DEV - 1, dtype=jnp.int32))[:GHOST - 2]
        picked = jnp.concatenate([jnp.array([0, NODE_DEV - 1], dtype=jnp.int32), middle])
        return jax.random.permutation(jax.random.fold_in(subkey, 7), picked)
    lists = jax.vmap(one_list)(keys)
    return lists.reshape(parts_count, 2, GHOST).transpose(1, 0, 2).reshape(2, parts_count * GHOST).astype(jnp.int32)


def steps_of(own_key, shape, pieces, low, top_value):
    def one(axis_at, shards_of):
        steps = jax.random.uniform(jax.random.fold_in(jax.random.fold_in(own_key, 6), axis_at), (shards_of,), jnp.float32, low / len(pieces), top_value / len(pieces))
        return jnp.repeat(jnp.exp(steps), shape[axis_at] // shards_of).reshape((-1,) + (1,) * (len(shape) - axis_at - 1))

    level = one(*pieces[0])
    for cut in pieces[1:]:
        level = level * one(*cut)
    return level


def bell_draw(own_key, extent, scale, bound, pieces=(), kind=jnp.bfloat16):
    gain = steps_of(own_key, extent, pieces, -0.22, 0.18) if pieces else 1.0
    result = jax.random.normal(own_key, extent, jnp.float32) * scale * gain
    return jnp.minimum(jnp.maximum(result, -bound), bound).astype(kind)


def setup_inputs(seed: int = 0) -> dict:
    splits = jax.random.split(jax.random.key(seed), 9)
    return {
        "action": bell_draw(splits[0], (NDIR, NFREQ, NODES), 1.0, 6.0, ((0, 4), (2, 64)), jnp.float32),
        "edge_angle": jnp.clip(jax.random.uniform(splits[1], (NEIGH, NODES), jnp.float32, -3.140625, 3.140625), -3.140625, 3.140625),
        "edge_speed": jnp.clip(jnp.exp(math.log(3.0) - 2.3025851 * jax.random.uniform(splits[2], (NEIGH, NODES), jnp.float32) ** steps_of(splits[2], (NEIGH, NODES), ((1, 64),), -0.2, 0.2)), 0.3, 3.0),
        "neighbours": draw_neighbours(jax.random.fold_in(splits[8], 71), 0),
        "send_rows": draw_send_rows(jax.random.fold_in(splits[8], 71), 0),
        "refract_rate": jnp.clip(jax.random.uniform(splits[5], (NFREQ, NODES), jnp.float32, -0.45, 0.45) * steps_of(splits[5], (NFREQ, NODES), ((1, 64),), -0.4, 0.0), -0.45, 0.45),
        "refract_angle": jnp.clip(jax.random.uniform(splits[6], (NODES,), jnp.float32, -3.140625, 3.140625), -3.140625, 3.140625),
        "shift_rate": jnp.clip(jax.random.uniform(splits[7], (NFREQ, NODES), jnp.float32, -0.45, 0.45) * steps_of(splits[7], (NFREQ, NODES), ((1, 64),), -0.4, 0.0), -0.45, 0.45),
    }


def reference(action, edge_angle, edge_speed, neighbours, send_rows, refract_rate, refract_angle, shift_rate):
    partition = jnp.arange(NODES, dtype=jnp.int32) // NODE_DEV
    offsets = (jnp.arange(N_DOM, dtype=jnp.int32) * NODE_DEV)[:, None]
    to_lower = send_rows[0].reshape(N_DOM, GHOST).astype(jnp.int32) + offsets
    to_upper = send_rows[1].reshape(N_DOM, GHOST).astype(jnp.int32) + offsets
    below = jnp.clip(partition - 1, 0, N_DOM - 1)[None, :]
    above = jnp.clip(partition + 1, 0, N_DOM - 1)[None, :]
    lower_index = to_upper[below, jnp.clip(neighbours - NODE_DEV, 0, GHOST - 1)]
    upper_index = to_lower[above, jnp.clip(neighbours - NODE_DEV - GHOST, 0, GHOST - 1)]
    own_index = partition[None, :] * NODE_DEV + jnp.clip(neighbours, 0, NODE_DEV - 1)
    is_own = neighbours < NODE_DEV
    is_lower = jnp.logical_and(neighbours >= NODE_DEV, neighbours < NODE_DEV + GHOST)
    source = jnp.where(is_own, own_index, jnp.where(is_lower, lower_index, upper_index)).astype(jnp.int32)
    valid = jnp.logical_or(is_own, jnp.logical_or(jnp.logical_and(is_lower, partition[None, :] > 0),
                                                  jnp.logical_and(neighbours >= NODE_DEV + GHOST, partition[None, :] < N_DOM - 1)))
    angles = (2.0 * math.pi) * jnp.arange(NDIR).astype(jnp.float32) / NDIR

    def sweep_one(inputs):
        plane, angle = inputs
        weight = edge_speed * jax.nn.relu(jnp.cos(angle - edge_angle))
        denominator = 1.0 + jnp.sum(weight, axis=0)
        field = plane
        for sweep in range(SWEEPS):
            total = plane
            for slot in range(NEIGH):
                picked = jnp.where(valid[slot][None, :], field[:, source[slot]], jnp.float32(0.0))
                total = total + weight[slot][None, :] * picked
            field = total / denominator[None, :]
        return field

    swept = lax.map(sweep_one, (action, angles))
    speed = refract_rate[None, :, :] * jnp.sin(angles[:, None, None] - refract_angle[None, None, :])
    refracted = swept - (jax.nn.relu(speed) * (swept - jnp.roll(swept, 1, 0))
                         + jnp.minimum(speed, 0.0) * (jnp.roll(swept, -1, 0) - swept))
    padded = jnp.pad(refracted, ((0, 0), (1, 1), (0, 0)))
    rate = shift_rate[None, :, :]
    return refracted - (jax.nn.relu(rate) * (refracted - padded[:, :-2, :])
                        + jnp.minimum(rate, 0.0) * (padded[:, 2:, :] - refracted))
```

```python
import math

import jax
import jax.numpy as jnp
from jax import lax
from jax.experimental import pallas as pl
from jax.experimental.pallas import tpu as pltpu
from jax.sharding import PartitionSpec as P

NDIR = 64
NEIGH = 6
LANES = 128
PAD = 8

F32 = jnp.float32
VMEM = pl.BlockSpec(memory_space=pltpu.VMEM)
SMEM = pl.BlockSpec(memory_space=pltpu.SMEM)
ANY = pl.BlockSpec(memory_space=pl.ANY)


def params():
    return pltpu.CompilerParams(vmem_limit_bytes=8 << 20)


def cost(flops, nbytes):
    return pl.CostEstimate(flops=flops, bytes_accessed=nbytes, transcendentals=0)


def low_half():
    return lax.broadcasted_iota(jnp.int32, (8, LANES), 0) < 4


def two_rows(ref, first, second, low):
    return jnp.where(low, ref[pl.ds(first + PAD, 8), :], ref[pl.ds(second + (PAD - 4), 8), :])


def rows_body(send, action, field, to_upper, to_lower, stage, sems):
    chunks = action.shape[0] // LANES
    nodes = action.shape[1]
    copies = []
    for c in range(chunks):
        copy = pltpu.make_async_copy(action.at[pl.ds(c * LANES, LANES), :], stage.at[c], sems.at[c])
        copy.start()
        copies.append(copy)
    for c in range(chunks):
        copies[c].wait()
        field[pl.ds(PAD + c, nodes, stride=4), :] = stage[c].T
    low = low_half()
    ghost = to_upper.shape[0] // 4
    for i in range(0, ghost, 2):
        to_upper[pl.ds(4 * i, 8), :] = two_rows(field, send[1, i] * 4, send[1, i + 1] * 4, low)
        to_lower[pl.ds(4 * i, 8), :] = two_rows(field, send[0, i] * 4, send[0, i + 1] * 4, low)


def weights_body(edge_angle, edge_speed, field, weight, base):
    sector = 16
    nodes = edge_angle.shape[1]
    freq = 4 * LANES // sector
    first = lax.axis_index("dir") * sector
    number = lax.broadcasted_iota(jnp.int32, (sector, nodes), 0) + first
    angle = (2.0 * math.pi) * number.astype(F32) / NDIR
    parts = []
    total = jnp.ones((sector, nodes), F32)
    for j in range(NEIGH):
        part = edge_speed[pl.ds(j, 1), :] * jnp.maximum(jnp.cos(angle - edge_angle[pl.ds(j, 1), :]), 0.0)
        parts.append(part)
        total = total + part
    inverse = 1.0 / total
    spread = (
        lax.broadcasted_iota(jnp.int32, (3 * sector, 4 * LANES), 0) % sector
        == lax.broadcasted_iota(jnp.int32, (3 * sector, 4 * LANES), 1) // freq
    ).astype(F32).astype(jnp.bfloat16)

    def widened(value):
        high = value.astype(jnp.bfloat16)
        rest = value - high.astype(F32)
        middle = rest.astype(jnp.bfloat16)
        last = (rest - middle.astype(F32)).astype(jnp.bfloat16)
        pieces = jnp.concatenate([high, middle, last], axis=0)
        return lax.dot_general(pieces, spread, (((0,), (0,)), ((), ())), preferred_element_type=F32)

    for j in range(NEIGH):
        wide = widened(parts[j] * inverse)
        for c in range(4):
            weight[pl.ds(PAD + j * 4 * nodes + c, nodes, stride=4), :] = wide[:, c * LANES : (c + 1) * LANES]
    wide = widened(inverse)
    for c in range(4):
        rows = pl.ds(PAD + c, nodes, stride=4)
        base[rows, :] = field[rows, :] * wide[:, c * LANES : (c + 1) * LANES]


def place_ghosts(field, lower, upper, nodes):
    part = lax.axis_index("dom")
    last = lax.axis_size("dom") - 1
    rows = lower.shape[0]
    field[pl.ds(PAD + 4 * nodes, rows), :] = jnp.where(part > 0, lower[...], 0.0)
    field[pl.ds(PAD + 4 * nodes + rows, rows), :] = jnp.where(part < last, upper[...], 0.0)


def shared_body(send, slots, field_in, lower, upper, weight, base, field, to_upper, to_lower):
    del field_in
    nodes = slots.shape[0] // NEIGH
    place_ghosts(field, lower, upper, nodes)
    low = low_half()
    ghost = to_upper.shape[0] // 4
    for row, out in ((1, to_upper), (0, to_lower)):
        for i in range(0, ghost, 2):
            n = send[row, i]
            m = send[row, i + 1]
            total = two_rows(base, n * 4, m * 4, low)
            for j in range(NEIGH):
                w = two_rows(weight, n * 4 + j * 4 * nodes, m * 4 + j * 4 * nodes, low)
                total = total + w * two_rows(field, slots[j * nodes + n], slots[j * nodes + m], low)
            out[pl.ds(4 * i, 8), :] = total


def sweep_rows(slots, field, weight, base, out, nodes, offset):
    low = low_half()

    def step(i, carry):
        n = i * 2
        row = pl.multiple_of(i * 8, 8)
        total = base[pl.ds(PAD + row, 8), :]
        for j in range(NEIGH):
            value = two_rows(field, slots[j * nodes + n], slots[j * nodes + n + 1], low)
            total = total + weight[pl.ds(PAD + j * 4 * nodes + row, 8), :] * value
        out[pl.ds(offset + row, 8), :] = total
        return carry

    lax.fori_loop(0, nodes // 2, step, 0, unroll=8)


def sweep_body(slots, field, weight, base, out):
    sweep_rows(slots, field, weight, base, out, slots.shape[0] // NEIGH, PAD)


def last_body(slots, field_in, lower, upper, weight, base, field, swept, first, last, rows):
    del field_in
    nodes = slots.shape[0] // NEIGH
    place_ghosts(field, lower, upper, nodes)
    sweep_rows(slots, field, weight, base, rows, nodes, 0)
    freq = first.shape[0]
    for c in range(4):
        planes = rows[pl.ds(c, nodes, stride=4), :].T
        swept[pl.ds(c * LANES, LANES), :] = planes
        if c == 0:
            first[...] = planes[:freq, :]
        if c == 3:
            last[...] = planes[LANES - freq :, :]


def finished(plane, before, after, direction, rate, bearing, shift):
    angle = (2.0 * math.pi) * direction.astype(F32) / NDIR
    speed = rate * jnp.sin(angle - bearing)
    value = plane - (jnp.maximum(speed, 0.0) * (plane - before) + jnp.minimum(speed, 0.0) * (after - plane))
    freq = plane.shape[0]
    row = lax.broadcasted_iota(jnp.int32, plane.shape, 0)
    under = jnp.where(row == 0, 0.0, pltpu.roll(value, 1, 0))
    over = jnp.where(row == freq - 1, 0.0, pltpu.roll(value, freq - 1, 0))
    return value - (jnp.maximum(shift, 0.0) * (value - under) + jnp.minimum(shift, 0.0) * (over - value))


def inner_body(swept, rate, bearing, shift, out, stage, sem):
    freq, nodes = rate.shape
    sector = swept.shape[0] // freq
    first = jnp.full((1, nodes), lax.axis_index("dir") * sector, jnp.int32)
    for d in range(1, sector - 1):
        plane = swept[pl.ds(d * freq, freq), :]
        stage[pl.ds((d - 1) * freq, freq), :] = finished(
            plane,
            swept[pl.ds((d - 1) * freq, freq), :],
            swept[pl.ds((d + 1) * freq, freq), :],
            first + d,
            rate[...],
            bearing[...],
            shift[...],
        )
    copy = pltpu.make_async_copy(stage, out.at[pl.ds(freq, (sector - 2) * freq), :], sem)
    copy.start()
    copy.wait()


def edge_body(swept, before, after, rate, bearing, shift, out_in, out, stage, sem):
    del out_in
    freq, nodes = rate.shape
    sector = swept.shape[0] // freq
    first = jnp.full((1, nodes), lax.axis_index("dir") * sector, jnp.int32)
    copies = []
    for k, d in enumerate((0, sector - 1)):
        plane = swept[pl.ds(d * freq, freq), :]
        low = before[...] if d == 0 else swept[pl.ds((d - 1) * freq, freq), :]
        high = after[...] if d == sector - 1 else swept[pl.ds((d + 1) * freq, freq), :]
        stage[k] = finished(plane, low, high, first + d, rate[...], bearing[...], shift[...])
        copy = pltpu.make_async_copy(stage.at[k], out.at[pl.ds(d * freq, freq), :], sem.at[k])
        copy.start()
        copies.append(copy)
    for copy in copies:
        copy.wait()


def around(array, axis, by):
    count = lax.axis_size(axis)
    return lax.ppermute(array, axis, [(i, (i + by) % count) for i in range(count)])


def shards(
    action, edge_angle, edge_speed, neighbours, send_rows, refract_rate, refract_angle, shift_rate
):
    sector, freq, nodes = action.shape
    ghost = send_rows.shape[1]
    field_rows = 4 * (nodes + 2 * ghost) + 2 * PAD
    fields = jax.ShapeDtypeStruct((field_rows, LANES), F32)
    shares = jax.ShapeDtypeStruct((4 * ghost, LANES), F32)
    weights = jax.ShapeDtypeStruct((NEIGH * 4 * nodes + 2 * PAD, LANES), F32)
    bases = jax.ShapeDtypeStruct((4 * nodes + 2 * PAD, LANES), F32)
    columns = sector * freq
    slots = (neighbours * 4).reshape(-1)
    bearing = refract_angle.reshape(1, nodes)

    field, up, down = pl.pallas_call(
        rows_body,
        out_shape=(fields, shares, shares),
        in_specs=[SMEM, ANY],
        out_specs=(VMEM, VMEM, VMEM),
        scratch_shapes=[pltpu.VMEM((4, LANES, nodes), F32), pltpu.SemaphoreType.DMA((4,))],
        compiler_params=params(),
        name="rows",
    )(send_rows, action.reshape(columns, nodes))
    lower = around(up, "dom", 1)
    upper = around(down, "dom", -1)
    weight, base = pl.pallas_call(
        weights_body,
        out_shape=(weights, bases),
        in_specs=[VMEM] * 3,
        out_specs=(VMEM, VMEM),
        compiler_params=params(),
        cost_estimate=cost(1 << 30, 8 << 20),
        name="weights",
    )(edge_angle, edge_speed, field)

    for _ in range(2):
        field, up, down = pl.pallas_call(
            shared_body,
            out_shape=(fields, shares, shares),
            in_specs=[SMEM, SMEM] + [VMEM] * 5,
            out_specs=(VMEM, VMEM, VMEM),
            input_output_aliases={2: 0},
            compiler_params=params(),
            name="shared",
        )(send_rows, slots, field, lower, upper, weight, base)
        lower = around(up, "dom", 1)
        upper = around(down, "dom", -1)
        field = pl.pallas_call(
            sweep_body,
            out_shape=fields,
            in_specs=[SMEM] + [VMEM] * 3,
            out_specs=VMEM,
            compiler_params=params(),
            cost_estimate=cost(1 << 30, 8 << 20),
            name="sweep",
        )(slots, field, weight, base)

    edge = jax.ShapeDtypeStruct((freq, nodes), F32)
    plane_shape = jax.ShapeDtypeStruct((columns, nodes), F32)
    _, swept, first, last = pl.pallas_call(
        last_body,
        out_shape=(fields, plane_shape, edge, edge),
        in_specs=[SMEM] + [VMEM] * 5,
        out_specs=(VMEM,) * 4,
        input_output_aliases={1: 0},
        scratch_shapes=[pltpu.VMEM((4 * nodes, LANES), F32)],
        compiler_params=params(),
        name="last_sweep",
    )(slots, field, lower, upper, weight, base)
    before = around(last, "dir", 1)
    after = around(first, "dir", -1)
    out = pl.pallas_call(
        inner_body,
        out_shape=plane_shape,
        in_specs=[VMEM] * 4,
        out_specs=ANY,
        scratch_shapes=[pltpu.VMEM((columns - 2 * freq, nodes), F32), pltpu.SemaphoreType.DMA],
        compiler_params=params(),
        cost_estimate=cost(1 << 28, 2 << 20),
        name="inner_planes",
    )(swept, refract_rate, bearing, shift_rate)
    out = pl.pallas_call(
        edge_body,
        out_shape=plane_shape,
        in_specs=[VMEM] * 6 + [ANY],
        out_specs=ANY,
        input_output_aliases={6: 0},
        scratch_shapes=[pltpu.VMEM((2, freq, nodes), F32), pltpu.SemaphoreType.DMA((2,))],
        compiler_params=params(),
        name="edge_planes",
    )(swept, before, after, refract_rate, bearing, shift_rate, out)
    return out.reshape(sector, freq, nodes)


def solution(mesh):
    return jax.shard_map(
        shards,
        mesh=mesh,
        in_specs=(
            P("dir", None, "dom"),
            P(None, "dom"),
            P(None, "dom"),
            P(None, "dom"),
            P(None, "dom"),
            P(None, "dom"),
            P("dom"),
            P(None, "dom"),
        ),
        out_specs=P("dir", None, "dom"),
        check_vma=False,
    )
```

```python
import math

import jax
import jax.numpy as jnp
from jax import lax
from jax.experimental import pallas as pl
from jax.experimental.pallas import tpu as pltpu
from jax.sharding import PartitionSpec as P

NDIR = 64
NEIGH = 6
LANES = 128
PAD = 8

F32 = jnp.float32
VMEM = pl.BlockSpec(memory_space=pltpu.VMEM)
SMEM = pl.BlockSpec(memory_space=pltpu.SMEM)
ANY = pl.BlockSpec(memory_space=pl.ANY)
HBM = pl.BlockSpec(memory_space=pltpu.HBM)


def in_hbm(array):
    return pltpu.with_memory_space_constraint(array, pltpu.HBM)


def params():
    return pltpu.CompilerParams(vmem_limit_bytes=8 << 20)


def cost(flops, nbytes):
    return pl.CostEstimate(flops=flops, bytes_accessed=nbytes, transcendentals=0)


def low_half():
    return lax.broadcasted_iota(jnp.int32, (8, LANES), 0) < 4


def two_rows(ref, first, second, low):
    return jnp.where(low, ref[pl.ds(first + PAD, 8), :], ref[pl.ds(second + (PAD - 4), 8), :])


def odd(axis):
    return lax.axis_index(axis) % 2


def rows_body(send_hbm, action, field, to_far, to_near, stage, send, sems, send_sem):
    chunks = action.shape[0] // LANES
    nodes = action.shape[1]
    copies = []
    for c in range(chunks):
        copy = pltpu.make_async_copy(action.at[pl.ds(c * LANES, LANES), :], stage.at[c], sems.at[c])
        copy.start()
        copies.append(copy)
    listed = pltpu.make_async_copy(send_hbm, send, send_sem)
    listed.start()
    for c in range(chunks):
        copies[c].wait()
        field[pl.ds(PAD + c, nodes, stride=4), :] = stage[c].T
    listed.wait()
    low = low_half()
    far = odd("dom")
    ghost = to_far.shape[0] // 4
    for i in range(0, ghost, 2):
        to_far[pl.ds(4 * i, 8), :] = two_rows(field, send[far, i] * 4, send[far, i + 1] * 4, low)
        to_near[pl.ds(4 * i, 8), :] = two_rows(field, send[1 - far, i] * 4, send[1 - far, i + 1] * 4, low)


def weights_body(
    send, slots, angle_hbm, speed_hbm, field, weight, base, share_weight, share_base, share_slots,
    edge_angle, edge_speed, sems,
):
    arriving = [
        pltpu.make_async_copy(angle_hbm, edge_angle, sems.at[0]),
        pltpu.make_async_copy(speed_hbm, edge_speed, sems.at[1]),
    ]
    for copy in arriving:
        copy.start()
    for copy in arriving:
        copy.wait()
    sector = 16
    nodes = edge_angle.shape[1]
    freq = 4 * LANES // sector
    first = lax.axis_index("dir") * sector
    number = lax.broadcasted_iota(jnp.int32, (sector, nodes), 0) + first
    angle = (2.0 * math.pi) * number.astype(F32) / NDIR
    parts = []
    total = jnp.ones((sector, nodes), F32)
    for j in range(NEIGH):
        part = edge_speed[pl.ds(j, 1), :] * jnp.maximum(jnp.cos(angle - edge_angle[pl.ds(j, 1), :]), 0.0)
        parts.append(part)
        total = total + part
    inverse = 1.0 / total
    spread = (
        lax.broadcasted_iota(jnp.int32, (3 * sector, 4 * LANES), 0) % sector
        == lax.broadcasted_iota(jnp.int32, (3 * sector, 4 * LANES), 1) // freq
    ).astype(F32).astype(jnp.bfloat16)

    def widened(value):
        high = value.astype(jnp.bfloat16)
        rest = value - high.astype(F32)
        middle = rest.astype(jnp.bfloat16)
        last = (rest - middle.astype(F32)).astype(jnp.bfloat16)
        pieces = jnp.concatenate([high, middle, last], axis=0)
        return lax.dot_general(pieces, spread, (((0,), (0,)), ((), ())), preferred_element_type=F32)

    for j in range(NEIGH):
        wide = widened(parts[j] * inverse)
        for c in range(4):
            weight[pl.ds(PAD + j * 4 * nodes + c, nodes, stride=4), :] = wide[:, c * LANES : (c + 1) * LANES]
    wide = widened(inverse)
    for c in range(4):
        rows = pl.ds(PAD + c, nodes, stride=4)
        base[rows, :] = field[rows, :] * wide[:, c * LANES : (c + 1) * LANES]
    low = low_half()
    far = odd("dom")
    ghost = send.shape[1]
    for k, row in enumerate((far, 1 - far)):
        for i in range(0, ghost, 2):
            n = send[row, i]
            m = send[row, i + 1]
            s = k * ghost + i
            share_base[pl.ds(4 * s, 8), :] = two_rows(base, n * 4, m * 4, low)
            for j in range(NEIGH):
                skip = j * 4 * nodes
                share_weight[pl.ds((j * 2 * ghost + s) * 4, 8), :] = two_rows(weight, n * 4 + skip, m * 4 + skip, low)
                share_slots[j * 2 * ghost + s] = slots[j * nodes + n]
                share_slots[j * 2 * ghost + s + 1] = slots[j * nodes + m]


def place_ghosts(field, from_far, from_near, nodes):
    part = lax.axis_index("dom")
    last = lax.axis_size("dom") - 1
    rows = from_far.shape[0]
    start = PAD + 4 * nodes
    far = odd("dom")
    inside = jnp.logical_and(part > 0, part < last)
    field[pl.ds(pl.multiple_of(start + far * rows, 8), rows), :] = jnp.where(inside, from_far[...], 0.0)
    field[pl.ds(pl.multiple_of(start + (1 - far) * rows, 8), rows), :] = from_near[...]


def shared_body(slots, field_in, from_far, from_near, weight, base, field, to_far, to_near):
    del field_in
    ghost = to_far.shape[0] // 4
    nodes = (field.shape[0] - 2 * PAD) // 4 - 2 * ghost
    place_ghosts(field, from_far, from_near, nodes)
    low = low_half()
    for k, out in enumerate((to_far, to_near)):
        for i in range(0, ghost, 2):
            s = k * ghost + i
            total = base[pl.ds(4 * s, 8), :]
            for j in range(NEIGH):
                at = j * 2 * ghost + s
                total = total + weight[pl.ds(4 * at, 8), :] * two_rows(field, slots[at], slots[at + 1], low)
            out[pl.ds(4 * i, 8), :] = total


def sweep_rows(slots, field, weight, base, out, nodes, offset):
    low = low_half()

    def step(i, carry):
        n = i * 2
        row = pl.multiple_of(i * 8, 8)
        total = base[pl.ds(PAD + row, 8), :]
        for j in range(NEIGH):
            value = two_rows(field, slots[j * nodes + n], slots[j * nodes + n + 1], low)
            total = total + weight[pl.ds(PAD + j * 4 * nodes + row, 8), :] * value
        out[pl.ds(offset + row, 8), :] = total
        return carry

    lax.fori_loop(0, nodes // 2, step, 0, unroll=8)


def sweep_body(slots, field, weight, base, out):
    sweep_rows(slots, field, weight, base, out, slots.shape[0] // NEIGH, PAD)


def last_body(slots, field_in, from_far, from_near, weight, base, field, swept, to_far, to_near, rows):
    del field_in
    nodes = slots.shape[0] // NEIGH
    place_ghosts(field, from_far, from_near, nodes)
    sweep_rows(slots, field, weight, base, rows, nodes, 0)
    freq = to_far.shape[0]
    for c in range(4):
        swept[pl.ds(c * LANES, LANES), :] = rows[pl.ds(c, nodes, stride=4), :].T
    first = swept[pl.ds(0, freq), :]
    last = swept[pl.ds(swept.shape[0] - freq, freq), :]
    far = odd("dir") > 0
    to_far[...] = jnp.where(far, last, first)
    to_near[...] = jnp.where(far, first, last)


def finished(plane, before, after, direction, rate, bearing, shift):
    angle = (2.0 * math.pi) * direction.astype(F32) / NDIR
    speed = rate * jnp.sin(angle - bearing)
    value = plane - (jnp.maximum(speed, 0.0) * (plane - before) + jnp.minimum(speed, 0.0) * (after - plane))
    freq = plane.shape[0]
    row = lax.broadcasted_iota(jnp.int32, plane.shape, 0)
    under = jnp.where(row == 0, 0.0, pltpu.roll(value, 1, 0))
    over = jnp.where(row == freq - 1, 0.0, pltpu.roll(value, freq - 1, 0))
    return value - (jnp.maximum(shift, 0.0) * (value - under) + jnp.minimum(shift, 0.0) * (over - value))


def inner_body(swept, rate, bearing, shift, out, stage, sem):
    freq, nodes = rate.shape
    sector = swept.shape[0] // freq
    first = jnp.full((1, nodes), lax.axis_index("dir") * sector, jnp.int32)
    for d in range(1, sector - 1):
        plane = swept[pl.ds(d * freq, freq), :]
        stage[pl.ds((d - 1) * freq, freq), :] = finished(
            plane,
            swept[pl.ds((d - 1) * freq, freq), :],
            swept[pl.ds((d + 1) * freq, freq), :],
            first + d,
            rate[...],
            bearing[...],
            shift[...],
        )
    copy = pltpu.make_async_copy(stage, out.at[pl.ds(freq, (sector - 2) * freq), :], sem)
    copy.start()
    copy.wait()


def edge_body(swept, from_far, from_near, rate, bearing, shift, out_in, out, stage, sem):
    del out_in
    far = odd("dir") > 0
    freq, nodes = rate.shape
    sector = swept.shape[0] // freq
    first = jnp.full((1, nodes), lax.axis_index("dir") * sector, jnp.int32)
    copies = []
    for k, d in enumerate((0, sector - 1)):
        plane = swept[pl.ds(d * freq, freq), :]
        low = jnp.where(far, from_near[...], from_far[...]) if d == 0 else swept[pl.ds((d - 1) * freq, freq), :]
        high = jnp.where(far, from_far[...], from_near[...]) if d == sector - 1 else swept[pl.ds((d + 1) * freq, freq), :]
        stage[k] = finished(plane, low, high, first + d, rate[...], bearing[...], shift[...])
        copy = pltpu.make_async_copy(stage.at[k], out.at[pl.ds(d * freq, freq), :], sem.at[k])
        copy.start()
        copies.append(copy)
    for copy in copies:
        copy.wait()


def swap_far(array, axis, closed):
    count = lax.axis_size(axis)
    ends = [(count - 1, 0), (0, count - 1)] if closed else [(0, 0), (count - 1, count - 1)]
    pairs = [p for i in range(1, count - 1, 2) for p in ((i, i + 1), (i + 1, i))]
    return lax.ppermute(array, axis, pairs + ends)


def swap_near(array, axis):
    count = lax.axis_size(axis)
    return lax.ppermute(array, axis, [p for i in range(0, count, 2) for p in ((i, i + 1), (i + 1, i))])


def shards(
    action, edge_angle, edge_speed, neighbours, send_rows, refract_rate, refract_angle, shift_rate
):
    sector, freq, nodes = action.shape
    ghost = send_rows.shape[1]
    field_rows = 4 * (nodes + 2 * ghost) + 2 * PAD
    fields = jax.ShapeDtypeStruct((field_rows, LANES), F32)
    shares = jax.ShapeDtypeStruct((4 * ghost, LANES), F32)
    weights = jax.ShapeDtypeStruct((NEIGH * 4 * nodes + 2 * PAD, LANES), F32)
    bases = jax.ShapeDtypeStruct((4 * nodes + 2 * PAD, LANES), F32)
    columns = sector * freq
    slots = (neighbours * 4).reshape(-1)
    bearing = refract_angle.reshape(1, nodes)

    field, far, near = pl.pallas_call(
        rows_body,
        out_shape=(fields, shares, shares),
        in_specs=[HBM, HBM],
        out_specs=(VMEM, VMEM, VMEM),
        scratch_shapes=[
            pltpu.VMEM((4, LANES, nodes), F32),
            pltpu.SMEM((2, ghost), jnp.int32),
            pltpu.SemaphoreType.DMA((4,)),
            pltpu.SemaphoreType.DMA,
        ],
        compiler_params=params(),
        name="rows",
    )(in_hbm(send_rows), in_hbm(action.reshape(columns, nodes)))
    far = swap_far(far, "dom", False)
    near = swap_near(near, "dom")
    weight, base, share_weight, share_base, share_slots = pl.pallas_call(
        weights_body,
        out_shape=(
            weights,
            bases,
            jax.ShapeDtypeStruct((NEIGH * 8 * ghost, LANES), F32),
            jax.ShapeDtypeStruct((8 * ghost, LANES), F32),
            jax.ShapeDtypeStruct((NEIGH * 2 * ghost,), jnp.int32),
        ),
        in_specs=[SMEM, SMEM, HBM, HBM, VMEM],
        out_specs=(VMEM, VMEM, VMEM, VMEM, SMEM),
        scratch_shapes=[
            pltpu.VMEM((NEIGH, nodes), F32),
            pltpu.VMEM((NEIGH, nodes), F32),
            pltpu.SemaphoreType.DMA((2,)),
        ],
        compiler_params=params(),
        cost_estimate=cost(1 << 30, 8 << 20),
        name="weights",
    )(send_rows, slots, in_hbm(edge_angle), in_hbm(edge_speed), field)

    for _ in range(2):
        field, far, near = pl.pallas_call(
            shared_body,
            out_shape=(fields, shares, shares),
            in_specs=[SMEM] + [VMEM] * 5,
            out_specs=(VMEM, VMEM, VMEM),
            input_output_aliases={1: 0},
            compiler_params=params(),
            name="shared",
        )(share_slots, field, far, near, share_weight, share_base)
        far = swap_far(far, "dom", False)
        near = swap_near(near, "dom")
        field = pl.pallas_call(
            sweep_body,
            out_shape=fields,
            in_specs=[SMEM] + [VMEM] * 3,
            out_specs=VMEM,
            compiler_params=params(),
            cost_estimate=cost(1 << 30, 8 << 20),
            name="sweep",
        )(slots, field, weight, base)

    edge = jax.ShapeDtypeStruct((freq, nodes), F32)
    plane_shape = jax.ShapeDtypeStruct((columns, nodes), F32)
    _, swept, far_plane, near_plane = pl.pallas_call(
        last_body,
        out_shape=(fields, plane_shape, edge, edge),
        in_specs=[SMEM] + [VMEM] * 5,
        out_specs=(VMEM,) * 4,
        input_output_aliases={1: 0},
        scratch_shapes=[pltpu.VMEM((4 * nodes, LANES), F32)],
        compiler_params=params(),
        name="last_sweep",
    )(slots, field, far, near, weight, base)
    far_plane = swap_far(far_plane, "dir", True)
    near_plane = swap_near(near_plane, "dir")
    out = pl.pallas_call(
        inner_body,
        out_shape=plane_shape,
        in_specs=[VMEM] * 4,
        out_specs=ANY,
        scratch_shapes=[pltpu.VMEM((columns - 2 * freq, nodes), F32), pltpu.SemaphoreType.DMA],
        compiler_params=params(),
        cost_estimate=cost(1 << 28, 2 << 20),
        name="inner_planes",
    )(swept, refract_rate, bearing, shift_rate)
    out = pl.pallas_call(
        edge_body,
        out_shape=plane_shape,
        in_specs=[VMEM] * 6 + [ANY],
        out_specs=ANY,
        input_output_aliases={6: 0},
        scratch_shapes=[pltpu.VMEM((2, freq, nodes), F32), pltpu.SemaphoreType.DMA((2,))],
        compiler_params=params(),
        name="edge_planes",
    )(swept, far_plane, near_plane, refract_rate, bearing, shift_rate, out)
    return out.reshape(sector, freq, nodes)


def solution(mesh):
    return jax.shard_map(
        shards,
        mesh=mesh,
        in_specs=(
            P("dir", None, "dom"),
            P(None, "dom"),
            P(None, "dom"),
            P(None, "dom"),
            P(None, "dom"),
            P(None, "dom"),
            P("dom"),
            P(None, "dom"),
        ),
        out_specs=P("dir", None, "dom"),
        check_vma=False,
    )
```

```python
import math

import jax
import jax.numpy as jnp
from jax import lax
from jax.experimental import pallas as pl
from jax.experimental.pallas import tpu as pltpu
from jax.sharding import PartitionSpec as P

NDIR = 64
NEIGH = 6
LANES = 128
PAD = 8

F32 = jnp.float32
VMEM = pl.BlockSpec(memory_space=pltpu.VMEM)
SMEM = pl.BlockSpec(memory_space=pltpu.SMEM)
ANY = pl.BlockSpec(memory_space=pl.ANY)
HBM = pl.BlockSpec(memory_space=pltpu.HBM)


def in_hbm(array):
    return pltpu.with_memory_space_constraint(array, pltpu.HBM)


def params():
    return pltpu.CompilerParams(vmem_limit_bytes=8 << 20)


def cost(flops, nbytes):
    return pl.CostEstimate(flops=flops, bytes_accessed=nbytes, transcendentals=0)


def low_half():
    return lax.broadcasted_iota(jnp.int32, (8, LANES), 0) < 4


def two_rows(ref, first, second, low):
    return jnp.where(low, ref[pl.ds(first + PAD, 8), :], ref[pl.ds(second + (PAD - 4), 8), :])


def odd(axis):
    return lax.axis_index(axis) % 2


def rows_body(
    send_hbm, action, angle_hbm, speed_hbm, neighbours, field, to_far, to_near, edge_angle, edge_speed, slots,
    stage, send, listed, sems,
):
    chunks = action.shape[0] // LANES
    nodes = action.shape[1]
    copies = []
    for c in range(chunks):
        copy = pltpu.make_async_copy(action.at[pl.ds(c * LANES, LANES), :], stage.at[c], sems.at[c])
        copy.start()
        copies.append(copy)
    for k, (source, target) in enumerate(
        ((send_hbm, send), (angle_hbm, edge_angle), (speed_hbm, edge_speed), (neighbours, listed))
    ):
        copy = pltpu.make_async_copy(source, target, sems.at[chunks + k])
        copy.start()
        copies.append(copy)
    for c in range(chunks):
        copies[c].wait()
        field[pl.ds(PAD + c, nodes, stride=4), :] = stage[c].T
    for copy in copies[chunks:]:
        copy.wait()
    slots[...] = listed[...] * 4
    low = low_half()
    far = odd("dom")
    ghost = to_far.shape[0] // 4
    for i in range(0, ghost, 2):
        to_far[pl.ds(4 * i, 8), :] = two_rows(field, send[far, i] * 4, send[far, i + 1] * 4, low)
        to_near[pl.ds(4 * i, 8), :] = two_rows(field, send[1 - far, i] * 4, send[1 - far, i + 1] * 4, low)


def weights_body(
    send_hbm, slots, edge_angle, edge_speed, field, weight, base, share_weight, share_base, share_slots, send, sem
):
    listed = pltpu.make_async_copy(send_hbm, send, sem)
    listed.start()
    sector = 16
    nodes = edge_angle.shape[1]
    freq = 4 * LANES // sector
    first = lax.axis_index("dir") * sector
    number = lax.broadcasted_iota(jnp.int32, (sector, nodes), 0) + first
    angle = (2.0 * math.pi) * number.astype(F32) / NDIR
    parts = []
    total = jnp.ones((sector, nodes), F32)
    for j in range(NEIGH):
        part = edge_speed[pl.ds(j, 1), :] * jnp.maximum(jnp.cos(angle - edge_angle[pl.ds(j, 1), :]), 0.0)
        parts.append(part)
        total = total + part
    inverse = 1.0 / total
    spread = (
        lax.broadcasted_iota(jnp.int32, (3 * sector, 4 * LANES), 0) % sector
        == lax.broadcasted_iota(jnp.int32, (3 * sector, 4 * LANES), 1) // freq
    ).astype(F32).astype(jnp.bfloat16)

    def widened(value):
        high = value.astype(jnp.bfloat16)
        rest = value - high.astype(F32)
        middle = rest.astype(jnp.bfloat16)
        last = (rest - middle.astype(F32)).astype(jnp.bfloat16)
        pieces = jnp.concatenate([high, middle, last], axis=0)
        return lax.dot_general(pieces, spread, (((0,), (0,)), ((), ())), preferred_element_type=F32)

    for j in range(NEIGH):
        wide = widened(parts[j] * inverse)
        for c in range(4):
            weight[pl.ds(PAD + j * 4 * nodes + c, nodes, stride=4), :] = wide[:, c * LANES : (c + 1) * LANES]
    wide = widened(inverse)
    for c in range(4):
        rows = pl.ds(PAD + c, nodes, stride=4)
        base[rows, :] = field[rows, :] * wide[:, c * LANES : (c + 1) * LANES]
    listed.wait()
    low = low_half()
    far = odd("dom")
    ghost = send.shape[1]
    for k, row in enumerate((far, 1 - far)):
        for i in range(0, ghost, 2):
            n = send[row, i]
            m = send[row, i + 1]
            s = k * ghost + i
            share_base[pl.ds(4 * s, 8), :] = two_rows(base, n * 4, m * 4, low)
            for j in range(NEIGH):
                skip = j * 4 * nodes
                share_weight[pl.ds((j * 2 * ghost + s) * 4, 8), :] = two_rows(weight, n * 4 + skip, m * 4 + skip, low)
                share_slots[j * 2 * ghost + s] = slots[j, n]
                share_slots[j * 2 * ghost + s + 1] = slots[j, m]


def place_ghosts(field, from_far, from_near, nodes):
    part = lax.axis_index("dom")
    last = lax.axis_size("dom") - 1
    rows = from_far.shape[0]
    start = PAD + 4 * nodes
    far = odd("dom")
    inside = jnp.logical_and(part > 0, part < last)
    field[pl.ds(pl.multiple_of(start + far * rows, 8), rows), :] = jnp.where(inside, from_far[...], 0.0)
    field[pl.ds(pl.multiple_of(start + (1 - far) * rows, 8), rows), :] = from_near[...]


def shared_body(slots, field_in, from_far, from_near, weight, base, field, to_far, to_near):
    del field_in
    ghost = to_far.shape[0] // 4
    nodes = (field.shape[0] - 2 * PAD) // 4 - 2 * ghost
    place_ghosts(field, from_far, from_near, nodes)
    low = low_half()
    for k, out in enumerate((to_far, to_near)):
        for i in range(0, ghost, 2):
            s = k * ghost + i
            total = base[pl.ds(4 * s, 8), :]
            for j in range(NEIGH):
                at = j * 2 * ghost + s
                total = total + weight[pl.ds(4 * at, 8), :] * two_rows(field, slots[at], slots[at + 1], low)
            out[pl.ds(4 * i, 8), :] = total


def sweep_rows(slots, field, weight, base, out, nodes, offset):
    low = low_half()

    def step(i, carry):
        n = i * 2
        row = pl.multiple_of(i * 8, 8)
        total = base[pl.ds(PAD + row, 8), :]
        for j in range(NEIGH):
            value = two_rows(field, slots[j, n], slots[j, n + 1], low)
            total = total + weight[pl.ds(PAD + j * 4 * nodes + row, 8), :] * value
        out[pl.ds(offset + row, 8), :] = total
        return carry

    lax.fori_loop(0, nodes // 2, step, 0, unroll=8)


def sweep_body(slots, field, weight, base, out):
    sweep_rows(slots, field, weight, base, out, slots.shape[1], PAD)


def last_body(slots, field_in, from_far, from_near, weight, base, field, swept, to_far, to_near, rows):
    del field_in
    nodes = slots.shape[1]
    place_ghosts(field, from_far, from_near, nodes)
    sweep_rows(slots, field, weight, base, rows, nodes, 0)
    freq = to_far.shape[0]
    for c in range(4):
        swept[pl.ds(c * LANES, LANES), :] = rows[pl.ds(c, nodes, stride=4), :].T
    first = swept[pl.ds(0, freq), :]
    last = swept[pl.ds(swept.shape[0] - freq, freq), :]
    far = odd("dir") > 0
    to_far[...] = jnp.where(far, last, first)
    to_near[...] = jnp.where(far, first, last)


def finished(plane, before, after, direction, rate, bearing, shift):
    angle = (2.0 * math.pi) * direction.astype(F32) / NDIR
    speed = rate * jnp.sin(angle - bearing)
    value = plane - (jnp.maximum(speed, 0.0) * (plane - before) + jnp.minimum(speed, 0.0) * (after - plane))
    freq = plane.shape[0]
    row = lax.broadcasted_iota(jnp.int32, plane.shape, 0)
    under = jnp.where(row == 0, 0.0, pltpu.roll(value, 1, 0))
    over = jnp.where(row == freq - 1, 0.0, pltpu.roll(value, freq - 1, 0))
    return value - (jnp.maximum(shift, 0.0) * (value - under) + jnp.minimum(shift, 0.0) * (over - value))


def inner_body(swept, rate, bearing, shift, out, stage, sem):
    freq, nodes = rate.shape
    sector = swept.shape[0] // freq
    first = jnp.full((1, nodes), lax.axis_index("dir") * sector, jnp.int32)
    for d in range(1, sector - 1):
        plane = swept[pl.ds(d * freq, freq), :]
        stage[pl.ds((d - 1) * freq, freq), :] = finished(
            plane,
            swept[pl.ds((d - 1) * freq, freq), :],
            swept[pl.ds((d + 1) * freq, freq), :],
            first + d,
            rate[...],
            bearing[...],
            shift[...],
        )
    copy = pltpu.make_async_copy(stage, out.at[pl.ds(freq, (sector - 2) * freq), :], sem)
    copy.start()
    copy.wait()


def edge_body(swept, from_far, from_near, rate, bearing, shift, out_in, out, stage, sem):
    del out_in
    far = odd("dir") > 0
    freq, nodes = rate.shape
    sector = swept.shape[0] // freq
    first = jnp.full((1, nodes), lax.axis_index("dir") * sector, jnp.int32)
    copies = []
    for k, d in enumerate((0, sector - 1)):
        plane = swept[pl.ds(d * freq, freq), :]
        low = jnp.where(far, from_near[...], from_far[...]) if d == 0 else swept[pl.ds((d - 1) * freq, freq), :]
        high = jnp.where(far, from_far[...], from_near[...]) if d == sector - 1 else swept[pl.ds((d + 1) * freq, freq), :]
        stage[k] = finished(plane, low, high, first + d, rate[...], bearing[...], shift[...])
        copy = pltpu.make_async_copy(stage.at[k], out.at[pl.ds(d * freq, freq), :], sem.at[k])
        copy.start()
        copies.append(copy)
    for copy in copies:
        copy.wait()


def swap_far_parts(array):
    count, width = (lax.axis_size("dom"), lax.axis_size("dir"))
    pairs = []
    for d in range(width):
        for i in range(1, count - 1, 2):
            here, there = (i * width + d, (i + 1) * width + d)
            pairs += [(here, there), (there, here)]
        for i in (0, count - 1):
            pairs.append((i * width + d, i * width + (d ^ 1)))
    return lax.ppermute(array, ("dom", "dir"), pairs)


def swap_far_sectors(array):
    count = lax.axis_size("dir")
    pairs = [p for i in range(1, count, 2) for p in ((i, (i + 1) % count), ((i + 1) % count, i))]
    return lax.ppermute(array, "dir", pairs)


def swap_near(array, axis):
    count = lax.axis_size(axis)
    return lax.ppermute(array, axis, [p for i in range(0, count, 2) for p in ((i, i + 1), (i + 1, i))])


def shards(
    action, edge_angle, edge_speed, neighbours, send_rows, refract_rate, refract_angle, shift_rate
):
    sector, freq, nodes = action.shape
    ghost = send_rows.shape[1]
    field_rows = 4 * (nodes + 2 * ghost) + 2 * PAD
    fields = jax.ShapeDtypeStruct((field_rows, LANES), F32)
    shares = jax.ShapeDtypeStruct((4 * ghost, LANES), F32)
    weights = jax.ShapeDtypeStruct((NEIGH * 4 * nodes + 2 * PAD, LANES), F32)
    bases = jax.ShapeDtypeStruct((4 * nodes + 2 * PAD, LANES), F32)
    columns = sector * freq
    bearing = refract_angle.reshape(1, nodes)

    edges = jax.ShapeDtypeStruct((NEIGH, nodes), F32)
    field, far, near, angle, speed, slots = pl.pallas_call(
        rows_body,
        out_shape=(fields, shares, shares, edges, edges, jax.ShapeDtypeStruct((NEIGH, nodes), jnp.int32)),
        in_specs=[HBM] * 5,
        out_specs=(VMEM,) * 6,
        scratch_shapes=[
            pltpu.VMEM((4, LANES, nodes), F32),
            pltpu.SMEM((2, ghost), jnp.int32),
            pltpu.VMEM((NEIGH, nodes), jnp.int32),
            pltpu.SemaphoreType.DMA((8,)),
        ],
        compiler_params=params(),
        name="rows",
    )(*(in_hbm(x) for x in (send_rows, action.reshape(columns, nodes), edge_angle, edge_speed, neighbours)))
    far = swap_far_parts(far)
    near = swap_near(near, "dom")
    weight, base, share_weight, share_base, share_slots = pl.pallas_call(
        weights_body,
        out_shape=(
            weights,
            bases,
            jax.ShapeDtypeStruct((NEIGH * 8 * ghost, LANES), F32),
            jax.ShapeDtypeStruct((8 * ghost, LANES), F32),
            jax.ShapeDtypeStruct((NEIGH * 2 * ghost,), jnp.int32),
        ),
        in_specs=[HBM, SMEM] + [VMEM] * 3,
        out_specs=(VMEM, VMEM, VMEM, VMEM, SMEM),
        scratch_shapes=[pltpu.SMEM((2, ghost), jnp.int32), pltpu.SemaphoreType.DMA],
        compiler_params=params(),
        cost_estimate=cost(1 << 30, 8 << 20),
        name="weights",
    )(in_hbm(send_rows), slots, angle, speed, field)

    for _ in range(2):
        field, far, near = pl.pallas_call(
            shared_body,
            out_shape=(fields, shares, shares),
            in_specs=[SMEM] + [VMEM] * 5,
            out_specs=(VMEM, VMEM, VMEM),
            input_output_aliases={1: 0},
            compiler_params=params(),
            name="shared",
        )(share_slots, field, far, near, share_weight, share_base)
        far = swap_far_parts(far)
        near = swap_near(near, "dom")
        field = pl.pallas_call(
            sweep_body,
            out_shape=fields,
            in_specs=[SMEM] + [VMEM] * 3,
            out_specs=VMEM,
            compiler_params=params(),
            cost_estimate=cost(1 << 30, 8 << 20),
            name="sweep",
        )(slots, field, weight, base)

    edge = jax.ShapeDtypeStruct((freq, nodes), F32)
    plane_shape = jax.ShapeDtypeStruct((columns, nodes), F32)
    _, swept, far_plane, near_plane = pl.pallas_call(
        last_body,
        out_shape=(fields, plane_shape, edge, edge),
        in_specs=[SMEM] + [VMEM] * 5,
        out_specs=(VMEM,) * 4,
        input_output_aliases={1: 0},
        scratch_shapes=[pltpu.VMEM((4 * nodes, LANES), F32)],
        compiler_params=params(),
        name="last_sweep",
    )(slots, field, far, near, weight, base)
    far_plane = swap_far_sectors(far_plane)
    near_plane = swap_near(near_plane, "dir")
    out = pl.pallas_call(
        inner_body,
        out_shape=plane_shape,
        in_specs=[VMEM] * 4,
        out_specs=ANY,
        scratch_shapes=[pltpu.VMEM((columns - 2 * freq, nodes), F32), pltpu.SemaphoreType.DMA],
        compiler_params=params(),
        cost_estimate=cost(1 << 28, 2 << 20),
        name="inner_planes",
    )(swept, refract_rate, bearing, shift_rate)
    out = pl.pallas_call(
        edge_body,
        out_shape=plane_shape,
        in_specs=[VMEM] * 6 + [ANY],
        out_specs=ANY,
        input_output_aliases={6: 0},
        scratch_shapes=[pltpu.VMEM((2, freq, nodes), F32), pltpu.SemaphoreType.DMA((2,))],
        compiler_params=params(),
        name="edge_planes",
    )(swept, far_plane, near_plane, refract_rate, bearing, shift_rate, out)
    return out.reshape(sector, freq, nodes)


def solution(mesh):
    return jax.shard_map(
        shards,
        mesh=mesh,
        in_specs=(
            P("dir", None, "dom"),
            P(None, "dom"),
            P(None, "dom"),
            P(None, "dom"),
            P(None, "dom"),
            P(None, "dom"),
            P("dom"),
            P(None, "dom"),
        ),
        out_specs=P("dir", None, "dom"),
        check_vma=False,
    )
```

```python
import math

import jax
import jax.numpy as jnp
from jax import lax
from jax.experimental import pallas as pl
from jax.experimental.pallas import tpu as pltpu
from jax.sharding import PartitionSpec as P

NDIR = 64
NEIGH = 6
LANES = 128
PAD = 8

F32 = jnp.float32
VMEM = pl.BlockSpec(memory_space=pltpu.VMEM)
SMEM = pl.BlockSpec(memory_space=pltpu.SMEM)
ANY = pl.BlockSpec(memory_space=pl.ANY)
HBM = pl.BlockSpec(memory_space=pltpu.HBM)


def in_hbm(array):
    return pltpu.with_memory_space_constraint(array, pltpu.HBM)


def params():
    return pltpu.CompilerParams(vmem_limit_bytes=8 << 20)


def cost(flops, nbytes):
    return pl.CostEstimate(flops=flops, bytes_accessed=nbytes, transcendentals=0)


def low_half():
    return lax.broadcasted_iota(jnp.int32, (8, LANES), 0) < 4


def two_rows(ref, first, second, low):
    return jnp.where(low, ref[pl.ds(first + PAD, 8), :], ref[pl.ds(second + (PAD - 4), 8), :])


def odd(axis):
    return lax.axis_index(axis) % 2


def rows_body(
    send_hbm, action, angle_hbm, speed_hbm, neighbours, field, to_far, to_near, edge_angle, edge_speed, slots,
    stage, send, listed, sems,
):
    chunks = action.shape[0] // LANES
    nodes = action.shape[1]
    copies = []
    for c in range(chunks):
        copy = pltpu.make_async_copy(action.at[pl.ds(c * LANES, LANES), :], stage.at[c], sems.at[c])
        copy.start()
        copies.append(copy)
    for k, (source, target) in enumerate(
        ((send_hbm, send), (angle_hbm, edge_angle), (speed_hbm, edge_speed), (neighbours, listed))
    ):
        copy = pltpu.make_async_copy(source, target, sems.at[chunks + k])
        copy.start()
        copies.append(copy)
    for c in range(chunks):
        copies[c].wait()
        field[pl.ds(PAD + c, nodes, stride=4), :] = stage[c].T
    for copy in copies[chunks:]:
        copy.wait()
    for j in range(NEIGH):
        for c in range(nodes // LANES):
            at = j * (nodes // LANES) + c
            slots[pl.ds(at, 1), :] = listed[pl.ds(j, 1), c * LANES : (c + 1) * LANES] * 4
    low = low_half()
    far = odd("dom")
    ghost = to_far.shape[0] // 4
    for i in range(0, ghost, 2):
        to_far[pl.ds(4 * i, 8), :] = two_rows(field, send[far, i] * 4, send[far, i + 1] * 4, low)
        to_near[pl.ds(4 * i, 8), :] = two_rows(field, send[1 - far, i] * 4, send[1 - far, i + 1] * 4, low)


def weights_body(
    send_hbm, slots, edge_angle, edge_speed, field, weight, base, share_weight, share_base, share_slots, send, sem
):
    listed = pltpu.make_async_copy(send_hbm, send, sem)
    listed.start()
    sector = 16
    nodes = edge_angle.shape[1]
    freq = 4 * LANES // sector
    first = lax.axis_index("dir") * sector
    number = lax.broadcasted_iota(jnp.int32, (sector, nodes), 0) + first
    angle = (2.0 * math.pi) * number.astype(F32) / NDIR
    parts = []
    total = jnp.ones((sector, nodes), F32)
    for j in range(NEIGH):
        part = edge_speed[pl.ds(j, 1), :] * jnp.maximum(jnp.cos(angle - edge_angle[pl.ds(j, 1), :]), 0.0)
        parts.append(part)
        total = total + part
    inverse = 1.0 / total
    spread = (
        lax.broadcasted_iota(jnp.int32, (3 * sector, 4 * LANES), 0) % sector
        == lax.broadcasted_iota(jnp.int32, (3 * sector, 4 * LANES), 1) // freq
    ).astype(F32).astype(jnp.bfloat16)

    def widened(value):
        high = value.astype(jnp.bfloat16)
        rest = value - high.astype(F32)
        middle = rest.astype(jnp.bfloat16)
        last = (rest - middle.astype(F32)).astype(jnp.bfloat16)
        pieces = jnp.concatenate([high, middle, last], axis=0)
        return lax.dot_general(pieces, spread, (((0,), (0,)), ((), ())), preferred_element_type=F32)

    for j in range(NEIGH):
        wide = widened(parts[j] * inverse)
        for c in range(4):
            weight[pl.ds(PAD + j * 4 * nodes + c, nodes, stride=4), :] = wide[:, c * LANES : (c + 1) * LANES]
    wide = widened(inverse)
    for c in range(4):
        rows = pl.ds(PAD + c, nodes, stride=4)
        base[rows, :] = field[rows, :] * wide[:, c * LANES : (c + 1) * LANES]
    listed.wait()
    low = low_half()
    far = odd("dom")
    ghost = send.shape[1]
    for k, row in enumerate((far, 1 - far)):
        for i in range(0, ghost, 2):
            n = send[row, i]
            m = send[row, i + 1]
            s = k * ghost + i
            share_base[pl.ds(4 * s, 8), :] = two_rows(base, n * 4, m * 4, low)
            for j in range(NEIGH):
                skip = j * 4 * nodes
                share_weight[pl.ds((j * 2 * ghost + s) * 4, 8), :] = two_rows(weight, n * 4 + skip, m * 4 + skip, low)
                share_slots[j * 2 * ghost + s] = slots[j * nodes + n]
                share_slots[j * 2 * ghost + s + 1] = slots[j * nodes + m]


def place_ghosts(field, from_far, from_near, nodes):
    part = lax.axis_index("dom")
    last = lax.axis_size("dom") - 1
    rows = from_far.shape[0]
    start = PAD + 4 * nodes
    far = odd("dom")
    inside = jnp.logical_and(part > 0, part < last)
    field[pl.ds(pl.multiple_of(start + far * rows, 8), rows), :] = jnp.where(inside, from_far[...], 0.0)
    field[pl.ds(pl.multiple_of(start + (1 - far) * rows, 8), rows), :] = from_near[...]


def shared_body(slots, field_in, from_far, from_near, weight, base, field, to_far, to_near):
    del field_in
    ghost = to_far.shape[0] // 4
    nodes = (field.shape[0] - 2 * PAD) // 4 - 2 * ghost
    place_ghosts(field, from_far, from_near, nodes)
    low = low_half()
    for k, out in enumerate((to_far, to_near)):
        for i in range(0, ghost, 2):
            s = k * ghost + i
            total = base[pl.ds(4 * s, 8), :]
            for j in range(NEIGH):
                at = j * 2 * ghost + s
                total = total + weight[pl.ds(4 * at, 8), :] * two_rows(field, slots[at], slots[at + 1], low)
            out[pl.ds(4 * i, 8), :] = total


def sweep_rows(slots, field, weight, base, out, nodes, offset):
    low = low_half()

    def step(i, carry):
        n = i * 2
        row = pl.multiple_of(i * 8, 8)
        total = base[pl.ds(PAD + row, 8), :]
        for j in range(NEIGH):
            value = two_rows(field, slots[j * nodes + n], slots[j * nodes + n + 1], low)
            total = total + weight[pl.ds(PAD + j * 4 * nodes + row, 8), :] * value
        out[pl.ds(offset + row, 8), :] = total
        return carry

    lax.fori_loop(0, nodes // 2, step, 0, unroll=8)


def sweep_body(slots, field, weight, base, out):
    sweep_rows(slots, field, weight, base, out, slots.shape[0] // NEIGH, PAD)


def last_body(slots, field_in, from_far, from_near, weight, base, field, rows, to_far, to_near):
    del field_in
    nodes = slots.shape[0] // NEIGH
    place_ghosts(field, from_far, from_near, nodes)
    sweep_rows(slots, field, weight, base, rows, nodes, 0)
    freq = to_far.shape[0]
    first = rows[pl.ds(0, nodes, stride=4), :].T[:freq, :]
    last = rows[pl.ds(3, nodes, stride=4), :].T[LANES - freq :, :]
    far = odd("dir") > 0
    to_far[...] = jnp.where(far, last, first)
    to_near[...] = jnp.where(far, first, last)


def finished(plane, before, after, direction, rate, bearing, shift):
    angle = (2.0 * math.pi) * direction.astype(F32) / NDIR
    speed = rate * jnp.sin(angle - bearing)
    value = plane - (jnp.maximum(speed, 0.0) * (plane - before) + jnp.minimum(speed, 0.0) * (after - plane))
    freq = plane.shape[0]
    row = lax.broadcasted_iota(jnp.int32, plane.shape, 0)
    under = jnp.where(row == 0, 0.0, pltpu.roll(value, 1, 0))
    over = jnp.where(row == freq - 1, 0.0, pltpu.roll(value, freq - 1, 0))
    return value - (jnp.maximum(shift, 0.0) * (value - under) + jnp.minimum(shift, 0.0) * (over - value))


def inner_body(rows, rate, bearing, shift, out, ends, swept, stage, sems):
    freq, nodes = rate.shape
    chunks = swept.shape[0] // LANES
    width = LANES // freq
    sector = chunks * width
    first = jnp.full((1, nodes), lax.axis_index("dir") * sector, jnp.int32)
    copies = []
    done = 1
    for c in range(chunks):
        swept[pl.ds(c * LANES, LANES), :] = rows[pl.ds(c, nodes, stride=4), :].T
        until = (c + 1) * width - 1
        for d in range(done, until):
            stage[pl.ds((d - 1) * freq, freq), :] = finished(
                swept[pl.ds(d * freq, freq), :],
                swept[pl.ds((d - 1) * freq, freq), :],
                swept[pl.ds((d + 1) * freq, freq), :],
                first + d,
                rate[...],
                bearing[...],
                shift[...],
            )
        copy = pltpu.make_async_copy(
            stage.at[pl.ds((done - 1) * freq, (until - done) * freq), :],
            out.at[pl.ds(done * freq, (until - done) * freq), :],
            sems.at[c],
        )
        copy.start()
        copies.append(copy)
        done = until
    for k, d in enumerate((0, 1, sector - 2, sector - 1)):
        ends[k] = swept[pl.ds(d * freq, freq), :]
    for copy in copies:
        copy.wait()


def edge_body(ends, from_far, from_near, rate, bearing, shift, out_in, out, stage, sem):
    del out_in
    far = odd("dir") > 0
    freq, nodes = rate.shape
    sector = out.shape[0] // freq
    first = jnp.full((1, nodes), lax.axis_index("dir") * sector, jnp.int32)
    before = jnp.where(far, from_near[...], from_far[...])
    after = jnp.where(far, from_far[...], from_near[...])
    copies = []
    for k, (d, low, plane, high) in enumerate(
        ((0, before, ends[0], ends[1]), (sector - 1, ends[2], ends[3], after))
    ):
        stage[k] = finished(plane, low, high, first + d, rate[...], bearing[...], shift[...])
        copy = pltpu.make_async_copy(stage.at[k], out.at[pl.ds(d * freq, freq), :], sem.at[k])
        copy.start()
        copies.append(copy)
    for copy in copies:
        copy.wait()


def swap_far_parts(array):
    count, width = (lax.axis_size("dom"), lax.axis_size("dir"))
    pairs = []
    for d in range(width):
        for i in range(1, count - 1, 2):
            here, there = (i * width + d, (i + 1) * width + d)
            pairs += [(here, there), (there, here)]
        for i in (0, count - 1):
            pairs.append((i * width + d, i * width + (d ^ 1)))
    return lax.ppermute(array, ("dom", "dir"), pairs)


def swap_far_sectors(array):
    count = lax.axis_size("dir")
    pairs = [p for i in range(1, count, 2) for p in ((i, (i + 1) % count), ((i + 1) % count, i))]
    return lax.ppermute(array, "dir", pairs)


def swap_near(array, axis):
    count = lax.axis_size(axis)
    return lax.ppermute(array, axis, [p for i in range(0, count, 2) for p in ((i, i + 1), (i + 1, i))])


def shards(
    action, edge_angle, edge_speed, neighbours, send_rows, refract_rate, refract_angle, shift_rate
):
    sector, freq, nodes = action.shape
    ghost = send_rows.shape[1]
    field_rows = 4 * (nodes + 2 * ghost) + 2 * PAD
    fields = jax.ShapeDtypeStruct((field_rows, LANES), F32)
    shares = jax.ShapeDtypeStruct((4 * ghost, LANES), F32)
    weights = jax.ShapeDtypeStruct((NEIGH * 4 * nodes + 2 * PAD, LANES), F32)
    bases = jax.ShapeDtypeStruct((4 * nodes + 2 * PAD, LANES), F32)
    columns = sector * freq
    bearing = refract_angle.reshape(1, nodes)

    edges = jax.ShapeDtypeStruct((NEIGH, nodes), F32)
    field, far, near, angle, speed, slots = pl.pallas_call(
        rows_body,
        out_shape=(fields, shares, shares, edges, edges, jax.ShapeDtypeStruct((NEIGH * nodes // LANES, LANES), jnp.int32)),
        in_specs=[HBM] * 5,
        out_specs=(VMEM,) * 6,
        scratch_shapes=[
            pltpu.VMEM((4, LANES, nodes), F32),
            pltpu.SMEM((2, ghost), jnp.int32),
            pltpu.VMEM((NEIGH, nodes), jnp.int32),
            pltpu.SemaphoreType.DMA((8,)),
        ],
        compiler_params=params(),
        name="rows",
    )(*(in_hbm(x) for x in (send_rows, action.reshape(columns, nodes), edge_angle, edge_speed, neighbours)))
    slots = slots.reshape(-1)
    far = swap_far_parts(far)
    near = swap_near(near, "dom")
    weight, base, share_weight, share_base, share_slots = pl.pallas_call(
        weights_body,
        out_shape=(
            weights,
            bases,
            jax.ShapeDtypeStruct((NEIGH * 8 * ghost, LANES), F32),
            jax.ShapeDtypeStruct((8 * ghost, LANES), F32),
            jax.ShapeDtypeStruct((NEIGH * 2 * ghost,), jnp.int32),
        ),
        in_specs=[HBM, SMEM] + [VMEM] * 3,
        out_specs=(VMEM, VMEM, VMEM, VMEM, SMEM),
        scratch_shapes=[pltpu.SMEM((2, ghost), jnp.int32), pltpu.SemaphoreType.DMA],
        compiler_params=params(),
        cost_estimate=cost(1 << 30, 8 << 20),
        name="weights",
    )(in_hbm(send_rows), slots, angle, speed, field)

    for _ in range(2):
        field, far, near = pl.pallas_call(
            shared_body,
            out_shape=(fields, shares, shares),
            in_specs=[SMEM] + [VMEM] * 5,
            out_specs=(VMEM, VMEM, VMEM),
            input_output_aliases={1: 0},
            compiler_params=params(),
            name="shared",
        )(share_slots, field, far, near, share_weight, share_base)
        far = swap_far_parts(far)
        near = swap_near(near, "dom")
        field = pl.pallas_call(
            sweep_body,
            out_shape=fields,
            in_specs=[SMEM] + [VMEM] * 3,
            out_specs=VMEM,
            compiler_params=params(),
            cost_estimate=cost(1 << 30, 8 << 20),
            name="sweep",
        )(slots, field, weight, base)

    edge = jax.ShapeDtypeStruct((freq, nodes), F32)
    plane_shape = jax.ShapeDtypeStruct((columns, nodes), F32)
    _, rows, far_plane, near_plane = pl.pallas_call(
        last_body,
        out_shape=(fields, jax.ShapeDtypeStruct((4 * nodes, LANES), F32), edge, edge),
        in_specs=[SMEM] + [VMEM] * 5,
        out_specs=(VMEM,) * 4,
        input_output_aliases={1: 0},
        compiler_params=params(),
        name="last_sweep",
    )(slots, field, far, near, weight, base)
    far_plane = swap_far_sectors(far_plane)
    near_plane = swap_near(near_plane, "dir")
    out, ends = pl.pallas_call(
        inner_body,
        out_shape=(plane_shape, jax.ShapeDtypeStruct((4, freq, nodes), F32)),
        in_specs=[VMEM] * 4,
        out_specs=(ANY, VMEM),
        scratch_shapes=[
            pltpu.VMEM((columns, nodes), F32),
            pltpu.VMEM((columns - 2 * freq, nodes), F32),
            pltpu.SemaphoreType.DMA((4,)),
        ],
        compiler_params=params(),
        cost_estimate=cost(1 << 28, 2 << 20),
        name="inner_planes",
    )(rows, refract_rate, bearing, shift_rate)
    out = pl.pallas_call(
        edge_body,
        out_shape=plane_shape,
        in_specs=[VMEM] * 6 + [ANY],
        out_specs=ANY,
        input_output_aliases={6: 0},
        scratch_shapes=[pltpu.VMEM((2, freq, nodes), F32), pltpu.SemaphoreType.DMA((2,))],
        compiler_params=params(),
        name="edge_planes",
    )(ends, far_plane, near_plane, refract_rate, bearing, shift_rate, out)
    return out.reshape(sector, freq, nodes)


def solution(mesh):
    return jax.shard_map(
        shards,
        mesh=mesh,
        in_specs=(
            P("dir", None, "dom"),
            P(None, "dom"),
            P(None, "dom"),
            P(None, "dom"),
            P(None, "dom"),
            P(None, "dom"),
            P("dom"),
            P(None, "dom"),
        ),
        out_specs=P("dir", None, "dom"),
        check_vma=False,
    )
```

```python
import math

import jax
import jax.numpy as jnp
from jax import lax
from jax.experimental import pallas as pl
from jax.experimental.pallas import tpu as pltpu
from jax.sharding import PartitionSpec as P

NDIR = 64
NEIGH = 6
LANES = 128
EARLY = 12
PAD = 8

F32 = jnp.float32
VMEM = pl.BlockSpec(memory_space=pltpu.VMEM)
SMEM = pl.BlockSpec(memory_space=pltpu.SMEM)
ANY = pl.BlockSpec(memory_space=pl.ANY)
HBM = pl.BlockSpec(memory_space=pltpu.HBM)


def in_hbm(array):
    return pltpu.with_memory_space_constraint(array, pltpu.HBM)


def params():
    return pltpu.CompilerParams(vmem_limit_bytes=8 << 20)


def cost(flops, nbytes):
    return pl.CostEstimate(flops=flops, bytes_accessed=nbytes, transcendentals=0)


def low_half():
    return lax.broadcasted_iota(jnp.int32, (8, LANES), 0) < 4


def two_rows(ref, first, second, low):
    return jnp.where(low, ref[pl.ds(first + PAD, 8), :], ref[pl.ds(second + (PAD - 4), 8), :])


def odd(axis):
    return lax.axis_index(axis) % 2


def rows_body(
    send_hbm, action, angle_hbm, speed_hbm, neighbours, field, to_far, to_near, edge_angle, edge_speed, slots,
    stage, send, listed, sems,
):
    chunks = action.shape[0] // LANES
    nodes = action.shape[1]
    blocks = nodes // LANES
    copies = []
    for c in range(chunks):
        for b in range(blocks):
            k = c * blocks + b
            tile = action.at[pl.ds(c * LANES, LANES), pl.ds(b * LANES, LANES)]
            copies.append(pltpu.make_async_copy(tile, stage.at[k], sems.at[k]))
    for k, (source, target) in enumerate(
        ((send_hbm, send), (angle_hbm, edge_angle), (speed_hbm, edge_speed), (neighbours, listed))
    ):
        copies.append(pltpu.make_async_copy(source, target, sems.at[chunks * blocks + k]))
    for copy in copies:
        copy.start()
    for c in range(chunks):
        for b in range(blocks):
            k = c * blocks + b
            copies[k].wait()
            field[pl.ds(PAD + b * 4 * LANES + c, LANES, stride=4), :] = stage[k].T
    for copy in copies[chunks * blocks :]:
        copy.wait()
    for j in range(NEIGH):
        for b in range(blocks):
            slots[pl.ds(j * blocks + b, 1), :] = listed[pl.ds(j, 1), b * LANES : (b + 1) * LANES] * 4
    most = jnp.max(listed[...], axis=0, keepdims=True) * 4
    for b in range(blocks):
        own = most[:, b * LANES : (b + 1) * LANES]
        slots[pl.ds(NEIGH * blocks + b, 1), :] = jnp.maximum(own, pltpu.roll(own, LANES - 1, 1))
    low = low_half()
    far = odd("dom")
    ghost = to_far.shape[0] // 4
    for i in range(0, ghost, 2):
        to_far[pl.ds(4 * i, 8), :] = two_rows(field, send[far, i] * 4, send[far, i + 1] * 4, low)
        to_near[pl.ds(4 * i, 8), :] = two_rows(field, send[1 - far, i] * 4, send[1 - far, i + 1] * 4, low)


def weights_body(
    send_hbm, slots, edge_angle, edge_speed, field, weight, base, share_weight, share_base, share_slots, order, send, sem
):
    listed = pltpu.make_async_copy(send_hbm, send, sem)
    listed.start()
    sector = 16
    nodes = edge_angle.shape[1]
    freq = 4 * LANES // sector
    first = lax.axis_index("dir") * sector
    number = lax.broadcasted_iota(jnp.int32, (sector, nodes), 0) + first
    angle = (2.0 * math.pi) * number.astype(F32) / NDIR
    parts = []
    total = jnp.ones((sector, nodes), F32)
    for j in range(NEIGH):
        part = edge_speed[pl.ds(j, 1), :] * jnp.maximum(jnp.cos(angle - edge_angle[pl.ds(j, 1), :]), 0.0)
        parts.append(part)
        total = total + part
    inverse = 1.0 / total
    spread = (
        lax.broadcasted_iota(jnp.int32, (3 * sector, 4 * LANES), 0) % sector
        == lax.broadcasted_iota(jnp.int32, (3 * sector, 4 * LANES), 1) // freq
    ).astype(F32).astype(jnp.bfloat16)

    def widened(value):
        high = value.astype(jnp.bfloat16)
        rest = value - high.astype(F32)
        middle = rest.astype(jnp.bfloat16)
        last = (rest - middle.astype(F32)).astype(jnp.bfloat16)
        pieces = jnp.concatenate([high, middle, last], axis=0)
        return lax.dot_general(pieces, spread, (((0,), (0,)), ((), ())), preferred_element_type=F32)

    for j in range(NEIGH):
        wide = widened(parts[j] * inverse)
        for c in range(4):
            weight[pl.ds(PAD + j * 4 * nodes + c, nodes, stride=4), :] = wide[:, c * LANES : (c + 1) * LANES]
    wide = widened(inverse)
    for c in range(4):
        rows = pl.ds(PAD + c, nodes, stride=4)
        base[rows, :] = field[rows, :] * wide[:, c * LANES : (c + 1) * LANES]
    listed.wait()
    low = low_half()
    far = odd("dom")
    ghost = send.shape[1]
    for k, row in enumerate((far, 1 - far)):
        for i in range(0, ghost, 2):
            n = send[row, i]
            m = send[row, i + 1]
            s = k * ghost + i
            share_base[pl.ds(4 * s, 8), :] = two_rows(base, n * 4, m * 4, low)
            for j in range(NEIGH):
                skip = j * 4 * nodes
                share_weight[pl.ds((j * 2 * ghost + s) * 4, 8), :] = two_rows(weight, n * 4 + skip, m * 4 + skip, low)
                share_slots[j * 2 * ghost + s] = slots[j * nodes + n]
                share_slots[j * 2 * ghost + s + 1] = slots[j * nodes + m]

    pairs = nodes // 2

    def place(i, counts):
        own, other = counts
        shared = (slots[NEIGH * nodes + 2 * i] >= 4 * nodes).astype(jnp.int32)
        order[jnp.where(shared > 0, pairs - 1 - other, own)] = i
        return own + 1 - shared, other + shared

    own, _ = lax.fori_loop(0, pairs, place, (jnp.int32(0), jnp.int32(0)), unroll=8)
    order[pairs] = own


def place_ghosts(field, from_far, from_near, nodes):
    part = lax.axis_index("dom")
    last = lax.axis_size("dom") - 1
    rows = from_far.shape[0]
    start = PAD + 4 * nodes
    far = odd("dom")
    inside = jnp.logical_and(part > 0, part < last)
    field[pl.ds(pl.multiple_of(start + far * rows, 8), rows), :] = jnp.where(inside, from_far[...], 0.0)
    field[pl.ds(pl.multiple_of(start + (1 - far) * rows, 8), rows), :] = from_near[...]


def share_rows(slots, field, weight, base, out, first):
    low = low_half()
    ghost = out.shape[0] // 4
    for i in range(0, ghost, 2):
        s = first + i
        total = base[pl.ds(4 * s, 8), :]
        for j in range(NEIGH):
            at = j * 2 * ghost + s
            total = total + weight[pl.ds(4 * at, 8), :] * two_rows(field, slots[at], slots[at + 1], low)
        out[pl.ds(4 * i, 8), :] = total


def far_body(slots, field_in, from_far, from_near, weight, base, field, to_far):
    del field_in
    ghost = to_far.shape[0] // 4
    place_ghosts(field, from_far, from_near, (field.shape[0] - 2 * PAD) // 4 - 2 * ghost)
    share_rows(slots, field, weight, base, to_far, 0)


def near_body(slots, field, weight, base, to_near):
    share_rows(slots, field, weight, base, to_near, to_near.shape[0] // 4)


def pair_row(slots, field, weight, base, i, nodes, low):
    n = i * 2
    row = pl.multiple_of(i * 8, 8)
    total = base[pl.ds(PAD + row, 8), :]
    for j in range(NEIGH):
        value = two_rows(field, slots[j * nodes + n], slots[j * nodes + n + 1], low)
        total = total + weight[pl.ds(PAD + j * 4 * nodes + row, 8), :] * value
    return row, total


def sweep_body(slots, field, weight, base, out):
    low = low_half()
    nodes = (base.shape[0] - 2 * PAD) // 4

    def step(i, carry):
        row, total = pair_row(slots, field, weight, base, i, nodes, low)
        out[pl.ds(PAD + row, 8), :] = total
        return carry

    lax.fori_loop(0, nodes // 2, step, 0, unroll=8)


def listed_pairs(order, slots, field, weight, base, rows, first, until):
    low = low_half()
    nodes = rows.shape[0] // 4

    def step(g, carry):
        for u in range(8):
            row, total = pair_row(slots, field, weight, base, order[g * 8 + u], nodes, low)
            rows[pl.ds(row, 8), :] = total
        return carry

    lax.fori_loop(first, until, step, 0)


def early_groups(order, nodes):
    return jnp.minimum(order[nodes // 2] // 8, EARLY)


def early_body(order, slots, field, weight, base, rows):
    listed_pairs(order, slots, field, weight, base, rows, 0, early_groups(order, rows.shape[0] // 4))


def last_body(order, slots, field_in, from_far, from_near, weight, base, rows_in, field, rows, to_far, to_near):
    del field_in, rows_in
    nodes = rows.shape[0] // 4
    place_ghosts(field, from_far, from_near, nodes)
    listed_pairs(order, slots, field, weight, base, rows, early_groups(order, nodes), nodes // 16)
    freq = to_far.shape[0]
    first = rows[pl.ds(0, nodes, stride=4), :].T[:freq, :]
    last = rows[pl.ds(3, nodes, stride=4), :].T[LANES - freq :, :]
    far = odd("dir") > 0
    to_far[...] = jnp.where(far, last, first)
    to_near[...] = jnp.where(far, first, last)


def finished(plane, before, after, direction, rate, bearing, shift):
    angle = (2.0 * math.pi) * direction.astype(F32) / NDIR
    speed = rate * jnp.sin(angle - bearing)
    value = plane - (jnp.maximum(speed, 0.0) * (plane - before) + jnp.minimum(speed, 0.0) * (after - plane))
    freq = plane.shape[0]
    row = lax.broadcasted_iota(jnp.int32, plane.shape, 0)
    under = jnp.where(row == 0, 0.0, pltpu.roll(value, 1, 0))
    over = jnp.where(row == freq - 1, 0.0, pltpu.roll(value, freq - 1, 0))
    return value - (jnp.maximum(shift, 0.0) * (value - under) + jnp.minimum(shift, 0.0) * (over - value))


def inner_body(rows, rate, bearing, shift, out, ends, swept, stage, sems):
    freq, nodes = rate.shape
    chunks = swept.shape[0] // LANES
    width = LANES // freq
    sector = chunks * width
    first = jnp.full((1, nodes), lax.axis_index("dir") * sector, jnp.int32)
    copies = []
    done = 1
    for c in range(chunks):
        swept[pl.ds(c * LANES, LANES), :] = rows[pl.ds(c, nodes, stride=4), :].T
        until = (c + 1) * width - 1
        for d in range(done, until):
            stage[pl.ds((d - 1) * freq, freq), :] = finished(
                swept[pl.ds(d * freq, freq), :],
                swept[pl.ds((d - 1) * freq, freq), :],
                swept[pl.ds((d + 1) * freq, freq), :],
                first + d,
                rate[...],
                bearing[...],
                shift[...],
            )
        copy = pltpu.make_async_copy(
            stage.at[pl.ds((done - 1) * freq, (until - done) * freq), :],
            out.at[pl.ds(done * freq, (until - done) * freq), :],
            sems.at[c],
        )
        copy.start()
        copies.append(copy)
        done = until
    for k, d in enumerate((0, 1, sector - 2, sector - 1)):
        ends[k] = swept[pl.ds(d * freq, freq), :]
    for copy in copies:
        copy.wait()


def edge_body(ends, from_far, from_near, rate, bearing, shift, out_in, out, stage, sem):
    del out_in
    far = odd("dir") > 0
    freq, nodes = rate.shape
    sector = out.shape[0] // freq
    first = jnp.full((1, nodes), lax.axis_index("dir") * sector, jnp.int32)
    before = jnp.where(far, from_near[...], from_far[...])
    after = jnp.where(far, from_far[...], from_near[...])
    copies = []
    for k, (d, low, plane, high) in enumerate(
        ((0, before, ends[0], ends[1]), (sector - 1, ends[2], ends[3], after))
    ):
        stage[k] = finished(plane, low, high, first + d, rate[...], bearing[...], shift[...])
        copy = pltpu.make_async_copy(stage.at[k], out.at[pl.ds(d * freq, freq), :], sem.at[k])
        copy.start()
        copies.append(copy)
    for copy in copies:
        copy.wait()


def swap_far_parts(array):
    count, width = (lax.axis_size("dom"), lax.axis_size("dir"))
    pairs = []
    for d in range(width):
        for i in range(1, count - 1, 2):
            here, there = (i * width + d, (i + 1) * width + d)
            pairs += [(here, there), (there, here)]
        for i in (0, count - 1):
            pairs.append((i * width + d, i * width + (d ^ 1)))
    return lax.ppermute(array, ("dom", "dir"), pairs)


def swap_far_sectors(array):
    count = lax.axis_size("dir")
    pairs = [p for i in range(1, count, 2) for p in ((i, (i + 1) % count), ((i + 1) % count, i))]
    return lax.ppermute(array, "dir", pairs)


def swap_near(array, axis):
    count = lax.axis_size(axis)
    return lax.ppermute(array, axis, [p for i in range(0, count, 2) for p in ((i, i + 1), (i + 1, i))])


def shards(
    action, edge_angle, edge_speed, neighbours, send_rows, refract_rate, refract_angle, shift_rate
):
    sector, freq, nodes = action.shape
    ghost = send_rows.shape[1]
    field_rows = 4 * (nodes + 2 * ghost) + 2 * PAD
    fields = jax.ShapeDtypeStruct((field_rows, LANES), F32)
    shares = jax.ShapeDtypeStruct((4 * ghost, LANES), F32)
    weights = jax.ShapeDtypeStruct((NEIGH * 4 * nodes + 2 * PAD, LANES), F32)
    bases = jax.ShapeDtypeStruct((4 * nodes + 2 * PAD, LANES), F32)
    columns = sector * freq
    bearing = refract_angle.reshape(1, nodes)

    edges = jax.ShapeDtypeStruct((NEIGH, nodes), F32)
    field, far, near, angle, speed, slots = pl.pallas_call(
        rows_body,
        out_shape=(fields, shares, shares, edges, edges, jax.ShapeDtypeStruct(((NEIGH + 2) * nodes // LANES, LANES), jnp.int32)),
        in_specs=[HBM] * 5,
        out_specs=(VMEM,) * 6,
        scratch_shapes=[
            pltpu.VMEM((columns // LANES * nodes // LANES, LANES, LANES), F32),
            pltpu.SMEM((2, ghost), jnp.int32),
            pltpu.VMEM((NEIGH, nodes), jnp.int32),
            pltpu.SemaphoreType.DMA((columns // LANES * nodes // LANES + 4,)),
        ],
        compiler_params=params(),
        name="rows",
    )(*(in_hbm(x) for x in (send_rows, action.reshape(columns, nodes), edge_angle, edge_speed, neighbours)))
    slots = slots.reshape(-1)
    far = swap_far_parts(far)
    near = swap_near(near, "dom")
    weight, base, share_weight, share_base, share_slots, order = pl.pallas_call(
        weights_body,
        out_shape=(
            weights,
            bases,
            jax.ShapeDtypeStruct((NEIGH * 8 * ghost, LANES), F32),
            jax.ShapeDtypeStruct((8 * ghost, LANES), F32),
            jax.ShapeDtypeStruct((NEIGH * 2 * ghost,), jnp.int32),
            jax.ShapeDtypeStruct((nodes // 2 + 8,), jnp.int32),
        ),
        in_specs=[HBM, SMEM] + [VMEM] * 3,
        out_specs=(VMEM, VMEM, VMEM, VMEM, SMEM, SMEM),
        scratch_shapes=[pltpu.SMEM((2, ghost), jnp.int32), pltpu.SemaphoreType.DMA],
        compiler_params=params(),
        cost_estimate=cost(1 << 30, 8 << 20),
        name="weights",
    )(in_hbm(send_rows), slots, angle, speed, field)

    for _ in range(2):
        field, far = pl.pallas_call(
            far_body,
            out_shape=(fields, shares),
            in_specs=[SMEM] + [VMEM] * 5,
            out_specs=(VMEM, VMEM),
            input_output_aliases={1: 0},
            compiler_params=params(),
            name="shared_far",
        )(share_slots, field, far, near, share_weight, share_base)
        far = swap_far_parts(far)
        near = pl.pallas_call(
            near_body,
            out_shape=shares,
            in_specs=[SMEM] + [VMEM] * 3,
            out_specs=VMEM,
            compiler_params=params(),
            cost_estimate=cost(1 << 27, 1 << 20),
            name="shared_near",
        )(share_slots, field, share_weight, share_base)
        near = swap_near(near, "dom")
        field = pl.pallas_call(
            sweep_body,
            out_shape=fields,
            in_specs=[SMEM] + [VMEM] * 3,
            out_specs=VMEM,
            compiler_params=params(),
            cost_estimate=cost(1 << 30, 8 << 20),
            name="sweep",
        )(slots, field, weight, base)

    edge = jax.ShapeDtypeStruct((freq, nodes), F32)
    plane_shape = jax.ShapeDtypeStruct((columns, nodes), F32)
    swept_rows = jax.ShapeDtypeStruct((4 * nodes, LANES), F32)
    rows = pl.pallas_call(
        early_body,
        out_shape=swept_rows,
        in_specs=[SMEM, SMEM] + [VMEM] * 3,
        out_specs=VMEM,
        compiler_params=params(),
        cost_estimate=cost(1 << 29, 4 << 20),
        name="last_sweep_early",
    )(order, slots, field, weight, base)
    _, rows, far_plane, near_plane = pl.pallas_call(
        last_body,
        out_shape=(fields, swept_rows, edge, edge),
        in_specs=[SMEM, SMEM] + [VMEM] * 6,
        out_specs=(VMEM,) * 4,
        input_output_aliases={2: 0, 7: 1},
        compiler_params=params(),
        name="last_sweep",
    )(order, slots, field, far, near, weight, base, rows)
    far_plane = swap_far_sectors(far_plane)
    near_plane = swap_near(near_plane, "dir")
    out, ends = pl.pallas_call(
        inner_body,
        out_shape=(plane_shape, jax.ShapeDtypeStruct((4, freq, nodes), F32)),
        in_specs=[VMEM] * 4,
        out_specs=(ANY, VMEM),
        scratch_shapes=[
            pltpu.VMEM((columns, nodes), F32),
            pltpu.VMEM((columns - 2 * freq, nodes), F32),
            pltpu.SemaphoreType.DMA((4,)),
        ],
        compiler_params=params(),
        cost_estimate=cost(1 << 28, 2 << 20),
        name="inner_planes",
    )(rows, refract_rate, bearing, shift_rate)
    out = pl.pallas_call(
        edge_body,
        out_shape=plane_shape,
        in_specs=[VMEM] * 6 + [ANY],
        out_specs=ANY,
        input_output_aliases={6: 0},
        scratch_shapes=[pltpu.VMEM((2, freq, nodes), F32), pltpu.SemaphoreType.DMA((2,))],
        compiler_params=params(),
        name="edge_planes",
    )(ends, far_plane, near_plane, refract_rate, bearing, shift_rate, out)
    return out.reshape(sector, freq, nodes)


def solution(mesh):
    return jax.shard_map(
        shards,
        mesh=mesh,
        in_specs=(
            P("dir", None, "dom"),
            P(None, "dom"),
            P(None, "dom"),
            P(None, "dom"),
            P(None, "dom"),
            P(None, "dom"),
            P("dom"),
            P(None, "dom"),
        ),
        out_specs=P("dir", None, "dom"),
        check_vma=False,
    )
```

```python
import math

import jax
import jax.numpy as jnp
from jax import lax
from jax.experimental import pallas as pl
from jax.experimental.pallas import tpu as pltpu
from jax.sharding import PartitionSpec as P

NDIR = 64
NEIGH = 6
LANES = 128
EARLY = 14
PAD = 8

F32 = jnp.float32
VMEM = pl.BlockSpec(memory_space=pltpu.VMEM)
SMEM = pl.BlockSpec(memory_space=pltpu.SMEM)
ANY = pl.BlockSpec(memory_space=pl.ANY)
HBM = pl.BlockSpec(memory_space=pltpu.HBM)


def in_hbm(array):
    return pltpu.with_memory_space_constraint(array, pltpu.HBM)


def params():
    return pltpu.CompilerParams(vmem_limit_bytes=8 << 20)


def cost(flops, nbytes):
    return pl.CostEstimate(flops=flops, bytes_accessed=nbytes, transcendentals=0)


def low_half():
    return lax.broadcasted_iota(jnp.int32, (8, LANES), 0) < 4


def two_rows(ref, first, second, low):
    return jnp.where(low, ref[pl.ds(first + PAD, 8), :], ref[pl.ds(second + (PAD - 4), 8), :])


def odd(axis):
    return lax.axis_index(axis) % 2


def rows_body(
    send_hbm, action, angle_hbm, speed_hbm, neighbours, field, to_far, to_near, edge_angle, edge_speed, slots,
    stage, send, listed, sems,
):
    chunks = action.shape[0] // LANES
    nodes = action.shape[1]
    blocks = nodes // LANES
    copies = []
    for c in range(chunks):
        copies.append(pltpu.make_async_copy(action.at[pl.ds(c * LANES, LANES), :], stage.at[c], sems.at[c]))
    for k, (source, target) in enumerate(
        ((send_hbm, send), (angle_hbm, edge_angle), (speed_hbm, edge_speed), (neighbours, listed))
    ):
        copies.append(pltpu.make_async_copy(source, target, sems.at[chunks + k]))
    for copy in copies:
        copy.start()
    for c in range(chunks):
        copies[c].wait()
        field[pl.ds(PAD + c, nodes, stride=4), :] = stage[c].T
    for copy in copies[chunks:]:
        copy.wait()
    for j in range(NEIGH):
        for b in range(blocks):
            slots[pl.ds(j * blocks + b, 1), :] = listed[pl.ds(j, 1), b * LANES : (b + 1) * LANES] * 4
    most = jnp.max(listed[...], axis=0, keepdims=True) * 4
    for b in range(blocks):
        own = most[:, b * LANES : (b + 1) * LANES]
        slots[pl.ds(NEIGH * blocks + b, 1), :] = jnp.maximum(own, pltpu.roll(own, LANES - 1, 1))
    low = low_half()
    far = odd("dom")
    ghost = to_far.shape[0] // 4
    for i in range(0, ghost, 2):
        to_far[pl.ds(4 * i, 8), :] = two_rows(field, send[far, i] * 4, send[far, i + 1] * 4, low)
        to_near[pl.ds(4 * i, 8), :] = two_rows(field, send[1 - far, i] * 4, send[1 - far, i + 1] * 4, low)


def weights_body(
    send_hbm, listed, edge_angle, edge_speed, field,
    weight, base, share_weight, share_base, slots, share_slots, order, send, sems,
):
    rows = listed.shape[0]
    copies = [
        pltpu.make_async_copy(listed.at[r], slots.at[pl.ds(r * LANES, LANES)], sems.at[r]) for r in range(rows)
    ]
    copies.append(pltpu.make_async_copy(send_hbm, send, sems.at[rows]))
    for copy in copies:
        copy.start()
    sector = 16
    nodes = edge_angle.shape[1]
    freq = 4 * LANES // sector
    first = lax.axis_index("dir") * sector
    number = lax.broadcasted_iota(jnp.int32, (sector, nodes), 0) + first
    angle = (2.0 * math.pi) * number.astype(F32) / NDIR
    parts = []
    total = jnp.ones((sector, nodes), F32)
    for j in range(NEIGH):
        part = edge_speed[pl.ds(j, 1), :] * jnp.maximum(jnp.cos(angle - edge_angle[pl.ds(j, 1), :]), 0.0)
        parts.append(part)
        total = total + part
    inverse = 1.0 / total
    spread = (
        lax.broadcasted_iota(jnp.int32, (3 * sector, 4 * LANES), 0) % sector
        == lax.broadcasted_iota(jnp.int32, (3 * sector, 4 * LANES), 1) // freq
    ).astype(F32).astype(jnp.bfloat16)

    def widened(value):
        high = value.astype(jnp.bfloat16)
        rest = value - high.astype(F32)
        middle = rest.astype(jnp.bfloat16)
        last = (rest - middle.astype(F32)).astype(jnp.bfloat16)
        pieces = jnp.concatenate([high, middle, last], axis=0)
        return lax.dot_general(pieces, spread, (((0,), (0,)), ((), ())), preferred_element_type=F32)

    for j in range(NEIGH):
        wide = widened(parts[j] * inverse)
        for c in range(4):
            weight[pl.ds(PAD + j * 4 * nodes + c, nodes, stride=4), :] = wide[:, c * LANES : (c + 1) * LANES]
    wide = widened(inverse)
    for c in range(4):
        rows = pl.ds(PAD + c, nodes, stride=4)
        base[rows, :] = field[rows, :] * wide[:, c * LANES : (c + 1) * LANES]
    for copy in copies:
        copy.wait()
    low = low_half()
    far = odd("dom")
    ghost = send.shape[1]
    for k, row in enumerate((far, 1 - far)):
        for i in range(0, ghost, 2):
            n = send[row, i]
            m = send[row, i + 1]
            s = k * ghost + i
            share_base[pl.ds(4 * s, 8), :] = two_rows(base, n * 4, m * 4, low)
            for j in range(NEIGH):
                skip = j * 4 * nodes
                share_weight[pl.ds((j * 2 * ghost + s) * 4, 8), :] = two_rows(weight, n * 4 + skip, m * 4 + skip, low)
                share_slots[j * 2 * ghost + s] = slots[j * nodes + n]
                share_slots[j * 2 * ghost + s + 1] = slots[j * nodes + m]

    pairs = nodes // 2

    def place(i, counts):
        own, other = counts
        shared = (slots[NEIGH * nodes + 2 * i] >= 4 * nodes).astype(jnp.int32)
        order[jnp.where(shared > 0, pairs - 1 - other, own)] = i
        return own + 1 - shared, other + shared

    own, _ = lax.fori_loop(0, pairs, place, (jnp.int32(0), jnp.int32(0)), unroll=8)
    order[pairs] = own


def place_ghosts(field, from_far, from_near, nodes):
    part = lax.axis_index("dom")
    last = lax.axis_size("dom") - 1
    rows = from_far.shape[0]
    start = PAD + 4 * nodes
    far = odd("dom")
    inside = jnp.logical_and(part > 0, part < last)
    field[pl.ds(pl.multiple_of(start + far * rows, 8), rows), :] = jnp.where(inside, from_far[...], 0.0)
    field[pl.ds(pl.multiple_of(start + (1 - far) * rows, 8), rows), :] = from_near[...]


def share_rows(slots, field, weight, base, out, first):
    low = low_half()
    ghost = out.shape[0] // 4
    for i in range(0, ghost, 2):
        s = first + i
        total = base[pl.ds(4 * s, 8), :]
        for j in range(NEIGH):
            at = j * 2 * ghost + s
            total = total + weight[pl.ds(4 * at, 8), :] * two_rows(field, slots[at], slots[at + 1], low)
        out[pl.ds(4 * i, 8), :] = total


def shared_body(slots, field_in, from_far, from_near, weight, base, field, to_far, to_near):
    del field_in
    ghost = to_far.shape[0] // 4
    place_ghosts(field, from_far, from_near, (field.shape[0] - 2 * PAD) // 4 - 2 * ghost)
    share_rows(slots, field, weight, base, to_far, 0)
    share_rows(slots, field, weight, base, to_near, ghost)


def pair_row(slots, field, weight, base, i, nodes, low):
    n = i * 2
    row = pl.multiple_of(i * 8, 8)
    total = base[pl.ds(PAD + row, 8), :]
    for j in range(NEIGH):
        value = two_rows(field, slots[j * nodes + n], slots[j * nodes + n + 1], low)
        total = total + weight[pl.ds(PAD + j * 4 * nodes + row, 8), :] * value
    return row, total


def sweep_body(slots, field, weight, base, out):
    low = low_half()
    nodes = (base.shape[0] - 2 * PAD) // 4

    def step(i, carry):
        row, total = pair_row(slots, field, weight, base, i, nodes, low)
        out[pl.ds(PAD + row, 8), :] = total
        return carry

    lax.fori_loop(0, nodes // 2, step, 0, unroll=8)


def listed_pairs(order, slots, field, weight, base, rows, first, until):
    low = low_half()
    nodes = rows.shape[0] // 4

    def step(g, carry):
        for u in range(8):
            row, total = pair_row(slots, field, weight, base, order[g * 8 + u], nodes, low)
            rows[pl.ds(row, 8), :] = total
        return carry

    lax.fori_loop(first, until, step, 0)


def early_groups(order, nodes):
    return jnp.minimum(order[nodes // 2] // 8, EARLY)


def early_body(order, slots, field, weight, base, rows):
    listed_pairs(order, slots, field, weight, base, rows, 0, early_groups(order, rows.shape[0] // 4))


def last_body(order, slots, field_in, from_far, from_near, weight, base, rows_in, field, rows, to_far, to_near):
    del field_in, rows_in
    nodes = rows.shape[0] // 4
    place_ghosts(field, from_far, from_near, nodes)
    listed_pairs(order, slots, field, weight, base, rows, early_groups(order, nodes), nodes // 16)
    freq = to_far.shape[0]
    first = rows[pl.ds(0, nodes, stride=4), :].T[:freq, :]
    last = rows[pl.ds(3, nodes, stride=4), :].T[LANES - freq :, :]
    far = odd("dir") > 0
    to_far[...] = jnp.where(far, last, first)
    to_near[...] = jnp.where(far, first, last)


def finished(plane, before, after, direction, rate, bearing, shift):
    angle = (2.0 * math.pi) * direction.astype(F32) / NDIR
    speed = rate * jnp.sin(angle - bearing)
    value = plane - (jnp.maximum(speed, 0.0) * (plane - before) + jnp.minimum(speed, 0.0) * (after - plane))
    freq = plane.shape[0]
    row = lax.broadcasted_iota(jnp.int32, plane.shape, 0)
    under = jnp.where(row == 0, 0.0, pltpu.roll(value, 1, 0))
    over = jnp.where(row == freq - 1, 0.0, pltpu.roll(value, freq - 1, 0))
    return value - (jnp.maximum(shift, 0.0) * (value - under) + jnp.minimum(shift, 0.0) * (over - value))


def inner_body(rows, rate, bearing, shift, out, ends, swept, stage, sems):
    freq, nodes = rate.shape
    chunks = swept.shape[0] // LANES
    width = LANES // freq
    sector = chunks * width
    first = jnp.full((1, nodes), lax.axis_index("dir") * sector, jnp.int32)
    copies = []
    done = 1
    for c in range(chunks):
        swept[pl.ds(c * LANES, LANES), :] = rows[pl.ds(c, nodes, stride=4), :].T
        until = (c + 1) * width - 1
        for d in range(done, until):
            stage[pl.ds((d - 1) * freq, freq), :] = finished(
                swept[pl.ds(d * freq, freq), :],
                swept[pl.ds((d - 1) * freq, freq), :],
                swept[pl.ds((d + 1) * freq, freq), :],
                first + d,
                rate[...],
                bearing[...],
                shift[...],
            )
        copy = pltpu.make_async_copy(
            stage.at[pl.ds((done - 1) * freq, (until - done) * freq), :],
            out.at[pl.ds(done * freq, (until - done) * freq), :],
            sems.at[c],
        )
        copy.start()
        copies.append(copy)
        done = until
    for k, d in enumerate((0, 1, sector - 2, sector - 1)):
        ends[k] = swept[pl.ds(d * freq, freq), :]
    for copy in copies:
        copy.wait()


def edge_body(ends, from_far, from_near, rate, bearing, shift, out_in, out, stage, sem):
    del out_in
    far = odd("dir") > 0
    freq, nodes = rate.shape
    sector = out.shape[0] // freq
    first = jnp.full((1, nodes), lax.axis_index("dir") * sector, jnp.int32)
    before = jnp.where(far, from_near[...], from_far[...])
    after = jnp.where(far, from_far[...], from_near[...])
    copies = []
    for k, (d, low, plane, high) in enumerate(
        ((0, before, ends[0], ends[1]), (sector - 1, ends[2], ends[3], after))
    ):
        stage[k] = finished(plane, low, high, first + d, rate[...], bearing[...], shift[...])
        copy = pltpu.make_async_copy(stage.at[k], out.at[pl.ds(d * freq, freq), :], sem.at[k])
        copy.start()
        copies.append(copy)
    for copy in copies:
        copy.wait()


def swap_far_parts(array):
    count, width = (lax.axis_size("dom"), lax.axis_size("dir"))
    pairs = []
    for d in range(width):
        for i in range(1, count - 1, 2):
            here, there = (i * width + d, (i + 1) * width + d)
            pairs += [(here, there), (there, here)]
        for i in (0, count - 1):
            pairs.append((i * width + d, i * width + (d ^ 1)))
    return lax.ppermute(array, ("dom", "dir"), pairs)


def swap_far_sectors(array):
    count = lax.axis_size("dir")
    pairs = [p for i in range(1, count, 2) for p in ((i, (i + 1) % count), ((i + 1) % count, i))]
    return lax.ppermute(array, "dir", pairs)


def swap_near(array, axis):
    count = lax.axis_size(axis)
    return lax.ppermute(array, axis, [p for i in range(0, count, 2) for p in ((i, i + 1), (i + 1, i))])


def shards(
    action, edge_angle, edge_speed, neighbours, send_rows, refract_rate, refract_angle, shift_rate
):
    sector, freq, nodes = action.shape
    ghost = send_rows.shape[1]
    field_rows = 4 * (nodes + 2 * ghost) + 2 * PAD
    fields = jax.ShapeDtypeStruct((field_rows, LANES), F32)
    shares = jax.ShapeDtypeStruct((4 * ghost, LANES), F32)
    weights = jax.ShapeDtypeStruct((NEIGH * 4 * nodes + 2 * PAD, LANES), F32)
    bases = jax.ShapeDtypeStruct((4 * nodes + 2 * PAD, LANES), F32)
    columns = sector * freq
    bearing = refract_angle.reshape(1, nodes)

    edges = jax.ShapeDtypeStruct((NEIGH, nodes), F32)
    field, far, near, angle, speed, slots = pl.pallas_call(
        rows_body,
        out_shape=(fields, shares, shares, edges, edges, jax.ShapeDtypeStruct(((NEIGH + 2) * nodes // LANES, LANES), jnp.int32)),
        in_specs=[HBM] * 5,
        out_specs=(VMEM,) * 6,
        scratch_shapes=[
            pltpu.VMEM((columns // LANES, LANES, nodes), F32),
            pltpu.SMEM((2, ghost), jnp.int32),
            pltpu.VMEM((NEIGH, nodes), jnp.int32),
            pltpu.SemaphoreType.DMA((columns // LANES + 4,)),
        ],
        compiler_params=params(),
        name="rows",
    )(*(in_hbm(x) for x in (send_rows, action.reshape(columns, nodes), edge_angle, edge_speed, neighbours)))
    far = swap_far_parts(far)
    near = swap_near(near, "dom")
    weight, base, share_weight, share_base, slots, share_slots, order = pl.pallas_call(
        weights_body,
        out_shape=(
            weights,
            bases,
            jax.ShapeDtypeStruct((NEIGH * 8 * ghost, LANES), F32),
            jax.ShapeDtypeStruct((8 * ghost, LANES), F32),
            pltpu.SMEM(((NEIGH + 2) * nodes,), jnp.int32),
            pltpu.SMEM((NEIGH * 2 * ghost,), jnp.int32),
            pltpu.SMEM((nodes // 2 + 8,), jnp.int32),
        ),
        in_specs=[HBM] + [VMEM] * 4,
        out_specs=(VMEM,) * 4 + (SMEM,) * 3,
        scratch_shapes=[
            pltpu.SMEM((2, ghost), jnp.int32),
            pltpu.SemaphoreType.DMA(((NEIGH + 2) * nodes // LANES + 1,)),
        ],
        compiler_params=params(),
        cost_estimate=cost(1 << 30, 8 << 20),
        name="weights",
    )(in_hbm(send_rows), slots, angle, speed, field)

    for _ in range(2):
        field, far, near = pl.pallas_call(
            shared_body,
            out_shape=(fields, shares, shares),
            in_specs=[SMEM] + [VMEM] * 5,
            out_specs=(VMEM, VMEM, VMEM),
            input_output_aliases={1: 0},
            compiler_params=params(),
            name="shared",
        )(share_slots, field, far, near, share_weight, share_base)
        far = swap_far_parts(far)
        near = swap_near(near, "dom")
        field = pl.pallas_call(
            sweep_body,
            out_shape=fields,
            in_specs=[SMEM] + [VMEM] * 3,
            out_specs=VMEM,
            compiler_params=params(),
            cost_estimate=cost(1 << 30, 8 << 20),
            name="sweep",
        )(slots, field, weight, base)

    edge = jax.ShapeDtypeStruct((freq, nodes), F32)
    plane_shape = jax.ShapeDtypeStruct((columns, nodes), F32)
    swept_rows = jax.ShapeDtypeStruct((4 * nodes, LANES), F32)
    rows = pl.pallas_call(
        early_body,
        out_shape=swept_rows,
        in_specs=[SMEM, SMEM] + [VMEM] * 3,
        out_specs=VMEM,
        compiler_params=params(),
        cost_estimate=cost(1 << 29, 4 << 20),
        name="last_sweep_early",
    )(order, slots, field, weight, base)
    _, rows, far_plane, near_plane = pl.pallas_call(
        last_body,
        out_shape=(fields, swept_rows, edge, edge),
        in_specs=[SMEM, SMEM] + [VMEM] * 6,
        out_specs=(VMEM,) * 4,
        input_output_aliases={2: 0, 7: 1},
        compiler_params=params(),
        name="last_sweep",
    )(order, slots, field, far, near, weight, base, rows)
    far_plane = swap_far_sectors(far_plane)
    near_plane = swap_near(near_plane, "dir")
    out, ends = pl.pallas_call(
        inner_body,
        out_shape=(plane_shape, jax.ShapeDtypeStruct((4, freq, nodes), F32)),
        in_specs=[VMEM] * 4,
        out_specs=(ANY, VMEM),
        scratch_shapes=[
            pltpu.VMEM((columns, nodes), F32),
            pltpu.VMEM((columns - 2 * freq, nodes), F32),
            pltpu.SemaphoreType.DMA((4,)),
        ],
        compiler_params=params(),
        cost_estimate=cost(1 << 28, 2 << 20),
        name="inner_planes",
    )(rows, refract_rate, bearing, shift_rate)
    out = pl.pallas_call(
        edge_body,
        out_shape=plane_shape,
        in_specs=[VMEM] * 6 + [ANY],
        out_specs=ANY,
        input_output_aliases={6: 0},
        scratch_shapes=[pltpu.VMEM((2, freq, nodes), F32), pltpu.SemaphoreType.DMA((2,))],
        compiler_params=params(),
        name="edge_planes",
    )(ends, far_plane, near_plane, refract_rate, bearing, shift_rate, out)
    return out.reshape(sector, freq, nodes)


def solution(mesh):
    return jax.shard_map(
        shards,
        mesh=mesh,
        in_specs=(
            P("dir", None, "dom"),
            P(None, "dom"),
            P(None, "dom"),
            P(None, "dom"),
            P(None, "dom"),
            P(None, "dom"),
            P("dom"),
            P(None, "dom"),
        ),
        out_specs=P("dir", None, "dom"),
        check_vma=False,
    )
```

```python
import math

import jax
import jax.numpy as jnp
from jax import lax
from jax.experimental import pallas as pl
from jax.experimental.pallas import tpu as pltpu
from jax.sharding import PartitionSpec as P

NDIR = 64
NEIGH = 6
LANES = 128
GROUP = 16
EARLY = 7
PAD = 8

F32 = jnp.float32
VMEM = pl.BlockSpec(memory_space=pltpu.VMEM)
SMEM = pl.BlockSpec(memory_space=pltpu.SMEM)
ANY = pl.BlockSpec(memory_space=pl.ANY)
HBM = pl.BlockSpec(memory_space=pltpu.HBM)


def in_hbm(array):
    return pltpu.with_memory_space_constraint(array, pltpu.HBM)


def params():
    return pltpu.CompilerParams(vmem_limit_bytes=8 << 20)


def cost(flops, nbytes):
    return pl.CostEstimate(flops=flops, bytes_accessed=nbytes, transcendentals=0)


def low_half():
    return lax.broadcasted_iota(jnp.int32, (8, LANES), 0) < 4


def two_rows(ref, first, second, low):
    return jnp.where(low, ref[pl.ds(first + PAD, 8), :], ref[pl.ds(second + (PAD - 4), 8), :])


def odd(axis):
    return lax.axis_index(axis) % 2


def rows_body(
    send_hbm, action, angle_hbm, speed_hbm, neighbours, field, to_far, to_near, edge_angle, edge_speed, slots,
    stage, send, listed, sems,
):
    chunks = action.shape[0] // LANES
    nodes = action.shape[1]
    blocks = nodes // LANES
    copies = []
    for c in range(chunks):
        copies.append(pltpu.make_async_copy(action.at[pl.ds(c * LANES, LANES), :], stage.at[c], sems.at[c]))
    for k, (source, target) in enumerate(
        ((send_hbm, send), (angle_hbm, edge_angle), (speed_hbm, edge_speed), (neighbours, listed))
    ):
        copies.append(pltpu.make_async_copy(source, target, sems.at[chunks + k]))
    for copy in copies:
        copy.start()
    for c in range(chunks):
        copies[c].wait()
        field[pl.ds(PAD + c, nodes, stride=4), :] = stage[c].T
    for copy in copies[chunks:]:
        copy.wait()
    for j in range(NEIGH):
        for b in range(blocks):
            slots[pl.ds(j * blocks + b, 1), :] = listed[pl.ds(j, 1), b * LANES : (b + 1) * LANES] * 4
    most = jnp.max(listed[...], axis=0, keepdims=True) * 4
    for b in range(blocks):
        own = most[:, b * LANES : (b + 1) * LANES]
        slots[pl.ds(NEIGH * blocks + b, 1), :] = jnp.maximum(own, pltpu.roll(own, LANES - 1, 1))
    low = low_half()
    far = odd("dom")
    ghost = to_far.shape[0] // 4
    for i in range(0, ghost, 2):
        to_far[pl.ds(4 * i, 8), :] = two_rows(field, send[far, i] * 4, send[far, i + 1] * 4, low)
        to_near[pl.ds(4 * i, 8), :] = two_rows(field, send[1 - far, i] * 4, send[1 - far, i + 1] * 4, low)


def weights_body(
    send_hbm, listed, edge_angle, edge_speed, field,
    weight, base, share_weight, share_base, plane_weight, pick, slots, share_slots, order, send, sems,
):
    rows = listed.shape[0]
    copies = [
        pltpu.make_async_copy(listed.at[r], slots.at[pl.ds(r * LANES, LANES)], sems.at[r]) for r in range(rows)
    ]
    copies.append(pltpu.make_async_copy(send_hbm, send, sems.at[rows]))
    for copy in copies:
        copy.start()
    sector = 16
    nodes = edge_angle.shape[1]
    freq = 4 * LANES // sector
    first = lax.axis_index("dir") * sector
    number = lax.broadcasted_iota(jnp.int32, (sector, nodes), 0) + first
    angle = (2.0 * math.pi) * number.astype(F32) / NDIR
    parts = []
    total = jnp.ones((sector, nodes), F32)
    for j in range(NEIGH):
        part = edge_speed[pl.ds(j, 1), :] * jnp.maximum(jnp.cos(angle - edge_angle[pl.ds(j, 1), :]), 0.0)
        parts.append(part)
        total = total + part
    inverse = 1.0 / total
    spread = (
        lax.broadcasted_iota(jnp.int32, (3 * sector, 4 * LANES), 0) % sector
        == lax.broadcasted_iota(jnp.int32, (3 * sector, 4 * LANES), 1) // freq
    ).astype(F32).astype(jnp.bfloat16)

    def widened(value):
        high = value.astype(jnp.bfloat16)
        rest = value - high.astype(F32)
        middle = rest.astype(jnp.bfloat16)
        last = (rest - middle.astype(F32)).astype(jnp.bfloat16)
        pieces = jnp.concatenate([high, middle, last], axis=0)
        return lax.dot_general(pieces, spread, (((0,), (0,)), ((), ())), preferred_element_type=F32)

    ghost = send.shape[1]
    number = (lax.broadcasted_iota(jnp.int32, (2 * ghost, LANES), 0) + nodes) * 4
    blocks = nodes // LANES
    for j in range(NEIGH):
        for b in range(blocks):
            chosen = (number == listed[pl.ds(j * blocks + b, 1), :]).astype(F32).astype(jnp.bfloat16)
            pick[pl.ds(j * 6 * ghost, 6 * ghost), b * LANES : (b + 1) * LANES] = jnp.concatenate([chosen] * 3, axis=0)
        plane_weight[pl.ds(j * sector, sector), :] = parts[j] * inverse
        wide = widened(parts[j] * inverse)
        for c in range(4):
            weight[pl.ds(PAD + j * 4 * nodes + c, nodes, stride=4), :] = wide[:, c * LANES : (c + 1) * LANES]
    wide = widened(inverse)
    for c in range(4):
        rows = pl.ds(PAD + c, nodes, stride=4)
        base[rows, :] = field[rows, :] * wide[:, c * LANES : (c + 1) * LANES]
    for copy in copies:
        copy.wait()
    low = low_half()
    far = odd("dom")
    for k, row in enumerate((far, 1 - far)):
        for i in range(0, ghost, 2):
            n = send[row, i]
            m = send[row, i + 1]
            s = k * ghost + i
            share_base[pl.ds(4 * s, 8), :] = two_rows(base, n * 4, m * 4, low)
            for j in range(NEIGH):
                skip = j * 4 * nodes
                share_weight[pl.ds((j * 2 * ghost + s) * 4, 8), :] = two_rows(weight, n * 4 + skip, m * 4 + skip, low)
                share_slots[j * 2 * ghost + s] = slots[j * nodes + n]
                share_slots[j * 2 * ghost + s + 1] = slots[j * nodes + m]

    pairs = nodes // 2

    def place(i, counts):
        own, other = counts
        shared = (slots[NEIGH * nodes + 2 * i] >= 4 * nodes).astype(jnp.int32)
        order[jnp.where(shared > 0, pairs - 1 - other, own)] = i
        return own + 1 - shared, other + shared

    own, _ = lax.fori_loop(0, pairs, place, (jnp.int32(0), jnp.int32(0)), unroll=8)
    order[pairs] = own


def place_ghosts(field, from_far, from_near, nodes):
    part = lax.axis_index("dom")
    last = lax.axis_size("dom") - 1
    rows = from_far.shape[0]
    start = PAD + 4 * nodes
    far = odd("dom")
    inside = jnp.logical_and(part > 0, part < last)
    field[pl.ds(pl.multiple_of(start + far * rows, 8), rows), :] = jnp.where(inside, from_far[...], 0.0)
    field[pl.ds(pl.multiple_of(start + (1 - far) * rows, 8), rows), :] = from_near[...]


def share_rows(slots, field, weight, base, out, first):
    low = low_half()
    ghost = out.shape[0] // 4
    for i in range(0, ghost, 2):
        s = first + i
        total = base[pl.ds(4 * s, 8), :]
        for j in range(NEIGH):
            at = j * 2 * ghost + s
            total = total + weight[pl.ds(4 * at, 8), :] * two_rows(field, slots[at], slots[at + 1], low)
        out[pl.ds(4 * i, 8), :] = total


def shared_body(slots, field_in, from_far, from_near, weight, base, field, to_far, to_near):
    del field_in
    ghost = to_far.shape[0] // 4
    place_ghosts(field, from_far, from_near, (field.shape[0] - 2 * PAD) // 4 - 2 * ghost)
    share_rows(slots, field, weight, base, to_far, 0)
    share_rows(slots, field, weight, base, to_near, ghost)


def pair_row(slots, field, weight, base, i, nodes, low):
    n = i * 2
    row = pl.multiple_of(i * 8, 8)
    total = base[pl.ds(PAD + row, 8), :]
    for j in range(NEIGH):
        value = two_rows(field, slots[j * nodes + n], slots[j * nodes + n + 1], low)
        total = total + weight[pl.ds(PAD + j * 4 * nodes + row, 8), :] * value
    return row, total


def clear_ghosts(out, nodes):
    rows = out.shape[0] - 2 * PAD - 4 * nodes
    out[pl.ds(PAD + 4 * nodes, rows), :] = jnp.zeros((rows, LANES), F32)


def all_pairs(slots, field, weight, base, out, offset):
    low = low_half()
    nodes = (base.shape[0] - 2 * PAD) // 4

    def step(i, carry):
        row, total = pair_row(slots, field, weight, base, i, nodes, low)
        out[pl.ds(offset + row, 8), :] = total
        return carry

    lax.fori_loop(0, nodes // 2, step, 0, unroll=GROUP)


def listed_pairs(order, slots, field, weight, base, out, first, until):
    low = low_half()
    nodes = (base.shape[0] - 2 * PAD) // 4

    def step(g, carry):
        for u in range(GROUP):
            row, total = pair_row(slots, field, weight, base, order[g * GROUP + u], nodes, low)
            out[pl.ds(PAD + row, 8), :] = total
        return carry

    lax.fori_loop(first, until, step, 0)


def early_groups(order, nodes):
    return jnp.minimum(order[nodes // 2] // GROUP, EARLY)


def first_body(order, slots, field, weight, base, swept, second):
    nodes = (base.shape[0] - 2 * PAD) // 4
    all_pairs(slots, field, weight, base, swept, PAD)
    clear_ghosts(second, nodes)
    listed_pairs(order, slots, swept, weight, base, second, 0, early_groups(order, nodes))


def second_body(order, slots, field, weight, base, second_in, second, planes, rows):
    del second_in
    nodes = (base.shape[0] - 2 * PAD) // 4
    listed_pairs(order, slots, field, weight, base, second, early_groups(order, nodes), nodes // (2 * GROUP))
    all_pairs(slots, second, weight, base, rows, 0)
    for c in range(planes.shape[0] // LANES):
        planes[pl.ds(c * LANES, LANES), :] = rows[pl.ds(c, nodes, stride=4), :].T


def received_rows(from_far, from_near, c):
    count = from_far.shape[0] // 4
    part = lax.axis_index("dom")
    inside = jnp.logical_and(part > 0, part < lax.axis_size("dom") - 1)
    far = jnp.where(inside, from_far[pl.ds(c, count, stride=4), :], 0.0)
    near = from_near[pl.ds(c, count, stride=4), :]
    swap = odd("dom") > 0
    return jnp.concatenate([jnp.where(swap, near, far), jnp.where(swap, far, near)], axis=0)


def in_pieces(value):
    high = value.astype(jnp.bfloat16)
    rest = value - high.astype(F32)
    middle = rest.astype(jnp.bfloat16)
    last = (rest - middle.astype(F32)).astype(jnp.bfloat16)
    return jnp.concatenate([high, middle, last], axis=0)


def selected(pieces, pick, j):
    depth = pieces.shape[0]
    return lax.dot_general(
        pieces, pick[pl.ds(j * depth, depth), :], (((0,), (0,)), ((), ())), preferred_element_type=F32
    )


def arrive_body(from_far, from_near, pick, plane_weight, planes, to_far, to_near):
    freq = to_far.shape[0]
    sector = planes.shape[0] // freq
    rows = received_rows(from_far, from_near, 0)
    lane = lax.broadcasted_iota(jnp.int32, rows.shape, 1)
    pieces = in_pieces(jnp.where(lane < freq, rows, received_rows(from_far, from_near, 3)))
    first = planes[pl.ds(0, freq), :]
    last = planes[pl.ds((sector - 1) * freq, freq), :]
    for j in range(NEIGH):
        found = selected(pieces, pick, j)
        first = first + plane_weight[pl.ds(j * sector, 1), :] * found[:freq, :]
        last = last + plane_weight[pl.ds(j * sector + sector - 1, 1), :] * found[LANES - freq :, :]
    far = odd("dir") > 0
    to_far[...] = jnp.where(far, last, first)
    to_near[...] = jnp.where(far, first, last)


def finished(plane, before, after, direction, rate, bearing, shift):
    angle = (2.0 * math.pi) * direction.astype(F32) / NDIR
    speed = rate * jnp.sin(angle - bearing)
    value = plane - (jnp.maximum(speed, 0.0) * (plane - before) + jnp.minimum(speed, 0.0) * (after - plane))
    freq = plane.shape[0]
    row = lax.broadcasted_iota(jnp.int32, plane.shape, 0)
    under = jnp.where(row == 0, 0.0, pltpu.roll(value, 1, 0))
    over = jnp.where(row == freq - 1, 0.0, pltpu.roll(value, freq - 1, 0))
    return value - (jnp.maximum(shift, 0.0) * (value - under) + jnp.minimum(shift, 0.0) * (over - value))


def inner_body(
    from_far, from_near, pick, plane_weight, planes, rate, bearing, shift, out, ends, swept, stage, sems
):
    freq, nodes = rate.shape
    chunks = swept.shape[0] // LANES
    width = LANES // freq
    sector = chunks * width
    first = jnp.full((1, nodes), lax.axis_index("dir") * sector, jnp.int32)
    copies = []
    done = 1
    for c in range(chunks):
        pieces = in_pieces(received_rows(from_far, from_near, c))
        total = [planes[pl.ds((c * width + k) * freq, freq), :] for k in range(width)]
        for j in range(NEIGH):
            found = selected(pieces, pick, j)
            for k in range(width):
                w = plane_weight[pl.ds(j * sector + c * width + k, 1), :]
                total[k] = total[k] + w * found[k * freq : (k + 1) * freq, :]
        for k in range(width):
            swept[pl.ds((c * width + k) * freq, freq), :] = total[k]
        until = (c + 1) * width - 1
        for d in range(done, until):
            stage[pl.ds((d - 1) * freq, freq), :] = finished(
                swept[pl.ds(d * freq, freq), :],
                swept[pl.ds((d - 1) * freq, freq), :],
                swept[pl.ds((d + 1) * freq, freq), :],
                first + d,
                rate[...],
                bearing[...],
                shift[...],
            )
        copy = pltpu.make_async_copy(
            stage.at[pl.ds((done - 1) * freq, (until - done) * freq), :],
            out.at[pl.ds(done * freq, (until - done) * freq), :],
            sems.at[c],
        )
        copy.start()
        copies.append(copy)
        done = until
    for k, d in enumerate((0, 1, sector - 2, sector - 1)):
        ends[k] = swept[pl.ds(d * freq, freq), :]
    for copy in copies:
        copy.wait()


def edge_body(ends, from_far, from_near, rate, bearing, shift, out_in, out, stage, sem):
    del out_in
    far = odd("dir") > 0
    freq, nodes = rate.shape
    sector = out.shape[0] // freq
    first = jnp.full((1, nodes), lax.axis_index("dir") * sector, jnp.int32)
    before = jnp.where(far, from_near[...], from_far[...])
    after = jnp.where(far, from_far[...], from_near[...])
    copies = []
    for k, (d, low, plane, high) in enumerate(
        ((0, before, ends[0], ends[1]), (sector - 1, ends[2], ends[3], after))
    ):
        stage[k] = finished(plane, low, high, first + d, rate[...], bearing[...], shift[...])
        copy = pltpu.make_async_copy(stage.at[k], out.at[pl.ds(d * freq, freq), :], sem.at[k])
        copy.start()
        copies.append(copy)
    for copy in copies:
        copy.wait()


def swap_far_parts(array):
    count, width = (lax.axis_size("dom"), lax.axis_size("dir"))
    pairs = []
    for d in range(width):
        for i in range(1, count - 1, 2):
            here, there = (i * width + d, (i + 1) * width + d)
            pairs += [(here, there), (there, here)]
        for i in (0, count - 1):
            pairs.append((i * width + d, i * width + (d ^ 1)))
    return lax.ppermute(array, ("dom", "dir"), pairs)


def swap_far_sectors(array):
    count = lax.axis_size("dir")
    pairs = [p for i in range(1, count, 2) for p in ((i, (i + 1) % count), ((i + 1) % count, i))]
    return lax.ppermute(array, "dir", pairs)


def swap_near(array, axis):
    count = lax.axis_size(axis)
    return lax.ppermute(array, axis, [p for i in range(0, count, 2) for p in ((i, i + 1), (i + 1, i))])


def shards(
    action, edge_angle, edge_speed, neighbours, send_rows, refract_rate, refract_angle, shift_rate
):
    sector, freq, nodes = action.shape
    ghost = send_rows.shape[1]
    field_rows = 4 * (nodes + 2 * ghost) + 2 * PAD
    fields = jax.ShapeDtypeStruct((field_rows, LANES), F32)
    shares = jax.ShapeDtypeStruct((4 * ghost, LANES), F32)
    weights = jax.ShapeDtypeStruct((NEIGH * 4 * nodes + 2 * PAD, LANES), F32)
    bases = jax.ShapeDtypeStruct((4 * nodes + 2 * PAD, LANES), F32)
    columns = sector * freq
    bearing = refract_angle.reshape(1, nodes)

    edges = jax.ShapeDtypeStruct((NEIGH, nodes), F32)
    field, far, near, angle, speed, slots = pl.pallas_call(
        rows_body,
        out_shape=(fields, shares, shares, edges, edges, jax.ShapeDtypeStruct(((NEIGH + 2) * nodes // LANES, LANES), jnp.int32)),
        in_specs=[HBM] * 5,
        out_specs=(VMEM,) * 6,
        scratch_shapes=[
            pltpu.VMEM((columns // LANES, LANES, nodes), F32),
            pltpu.SMEM((2, ghost), jnp.int32),
            pltpu.VMEM((NEIGH, nodes), jnp.int32),
            pltpu.SemaphoreType.DMA((columns // LANES + 4,)),
        ],
        compiler_params=params(),
        name="rows",
    )(*(in_hbm(x) for x in (send_rows, action.reshape(columns, nodes), edge_angle, edge_speed, neighbours)))
    far = swap_far_parts(far)
    near = swap_near(near, "dom")
    weight, base, share_weight, share_base, plane_weight, pick, slots, share_slots, order = pl.pallas_call(
        weights_body,
        out_shape=(
            weights,
            bases,
            jax.ShapeDtypeStruct((NEIGH * 8 * ghost, LANES), F32),
            jax.ShapeDtypeStruct((8 * ghost, LANES), F32),
            jax.ShapeDtypeStruct((NEIGH * sector, nodes), F32),
            jax.ShapeDtypeStruct((NEIGH * 6 * ghost, nodes), jnp.bfloat16),
            pltpu.SMEM(((NEIGH + 2) * nodes,), jnp.int32),
            pltpu.SMEM((NEIGH * 2 * ghost,), jnp.int32),
            pltpu.SMEM((nodes // 2 + 8,), jnp.int32),
        ),
        in_specs=[HBM] + [VMEM] * 4,
        out_specs=(VMEM,) * 6 + (SMEM,) * 3,
        scratch_shapes=[
            pltpu.SMEM((2, ghost), jnp.int32),
            pltpu.SemaphoreType.DMA(((NEIGH + 2) * nodes // LANES + 1,)),
        ],
        compiler_params=params(),
        cost_estimate=cost(1 << 30, 8 << 20),
        name="weights",
    )(in_hbm(send_rows), slots, angle, speed, field)

    def shared(field, far, near):
        field, far, near = pl.pallas_call(
            shared_body,
            out_shape=(fields, shares, shares),
            in_specs=[SMEM] + [VMEM] * 5,
            out_specs=(VMEM, VMEM, VMEM),
            input_output_aliases={1: 0},
            compiler_params=params(),
            name="shared",
        )(share_slots, field, far, near, share_weight, share_base)
        return field, swap_far_parts(far), swap_near(near, "dom")

    field, far, near = shared(field, far, near)
    field, second = pl.pallas_call(
        first_body,
        out_shape=(fields, fields),
        in_specs=[SMEM, SMEM] + [VMEM] * 3,
        out_specs=(VMEM, VMEM),
        compiler_params=params(),
        cost_estimate=cost(1 << 30, 8 << 20),
        name="first_sweep",
    )(order, slots, field, weight, base)
    field, far, near = shared(field, far, near)
    _, planes = pl.pallas_call(
        second_body,
        out_shape=(fields, jax.ShapeDtypeStruct((columns, nodes), F32)),
        in_specs=[SMEM, SMEM] + [VMEM] * 4,
        out_specs=(VMEM, VMEM),
        input_output_aliases={5: 0},
        scratch_shapes=[pltpu.VMEM((4 * nodes, LANES), F32)],
        compiler_params=params(),
        cost_estimate=cost(1 << 31, 16 << 20),
        name="second_sweep",
    )(order, slots, field, weight, base, second)

    edge = jax.ShapeDtypeStruct((freq, nodes), F32)
    plane_shape = jax.ShapeDtypeStruct((columns, nodes), F32)
    far_plane, near_plane = pl.pallas_call(
        arrive_body,
        out_shape=(edge, edge),
        in_specs=[VMEM] * 5,
        out_specs=(VMEM, VMEM),
        compiler_params=params(),
        name="last_sweep_edges",
    )(far, near, pick, plane_weight, planes)
    far_plane = swap_far_sectors(far_plane)
    near_plane = swap_near(near_plane, "dir")
    out, ends = pl.pallas_call(
        inner_body,
        out_shape=(plane_shape, jax.ShapeDtypeStruct((4, freq, nodes), F32)),
        in_specs=[VMEM] * 8,
        out_specs=(ANY, VMEM),
        scratch_shapes=[
            pltpu.VMEM((columns, nodes), F32),
            pltpu.VMEM((columns - 2 * freq, nodes), F32),
            pltpu.SemaphoreType.DMA((4,)),
        ],
        compiler_params=params(),
        cost_estimate=cost(1 << 28, 2 << 20),
        name="inner_planes",
    )(far, near, pick, plane_weight, planes, refract_rate, bearing, shift_rate)
    out = pl.pallas_call(
        edge_body,
        out_shape=plane_shape,
        in_specs=[VMEM] * 6 + [ANY],
        out_specs=ANY,
        input_output_aliases={6: 0},
        scratch_shapes=[pltpu.VMEM((2, freq, nodes), F32), pltpu.SemaphoreType.DMA((2,))],
        compiler_params=params(),
        name="edge_planes",
    )(ends, far_plane, near_plane, refract_rate, bearing, shift_rate, out)
    return out.reshape(sector, freq, nodes)


def solution(mesh):
    return jax.shard_map(
        shards,
        mesh=mesh,
        in_specs=(
            P("dir", None, "dom"),
            P(None, "dom"),
            P(None, "dom"),
            P(None, "dom"),
            P(None, "dom"),
            P(None, "dom"),
            P("dom"),
            P(None, "dom"),
        ),
        out_specs=P("dir", None, "dom"),
        check_vma=False,
    )
```

```python
import math

import jax
import jax.numpy as jnp
from jax import lax
from jax.experimental import pallas as pl
from jax.experimental.pallas import tpu as pltpu
from jax.sharding import PartitionSpec as P

NDIR = 64
NEIGH = 6
LANES = 128
GROUP = 16
EARLY = 7
PAD = 8

F32 = jnp.float32
VMEM = pl.BlockSpec(memory_space=pltpu.VMEM)
SMEM = pl.BlockSpec(memory_space=pltpu.SMEM)
ANY = pl.BlockSpec(memory_space=pl.ANY)
HBM = pl.BlockSpec(memory_space=pltpu.HBM)


def in_hbm(array):
    return pltpu.with_memory_space_constraint(array, pltpu.HBM)


def params():
    return pltpu.CompilerParams(vmem_limit_bytes=8 << 20)


def cost(flops, nbytes):
    return pl.CostEstimate(flops=flops, bytes_accessed=nbytes, transcendentals=0)


def low_half():
    return lax.broadcasted_iota(jnp.int32, (8, LANES), 0) < 4


def two_rows(ref, first, second, low):
    return jnp.where(low, ref[pl.ds(first + PAD, 8), :], ref[pl.ds(second + (PAD - 4), 8), :])


def odd(axis):
    return lax.axis_index(axis) % 2


def rows_body(
    send_hbm, action, angle_hbm, speed_hbm, neighbours, field, to_far, to_near, edge_angle, edge_speed, slots,
    stage, send, listed, sems,
):
    chunks = action.shape[0] // LANES
    nodes = action.shape[1]
    blocks = nodes // LANES
    copies = []
    for c in range(chunks):
        copies.append(pltpu.make_async_copy(action.at[pl.ds(c * LANES, LANES), :], stage.at[c], sems.at[c]))
    for k, (source, target) in enumerate(
        ((send_hbm, send), (angle_hbm, edge_angle), (speed_hbm, edge_speed), (neighbours, listed))
    ):
        copies.append(pltpu.make_async_copy(source, target, sems.at[chunks + k]))
    for copy in copies:
        copy.start()
    for c in range(chunks):
        copies[c].wait()
        field[pl.ds(PAD + c, nodes, stride=4), :] = stage[c].T
    for copy in copies[chunks:]:
        copy.wait()
    for j in range(NEIGH):
        for b in range(blocks):
            slots[pl.ds(j * blocks + b, 1), :] = listed[pl.ds(j, 1), b * LANES : (b + 1) * LANES] * 4
    most = jnp.max(listed[...], axis=0, keepdims=True) * 4
    for b in range(blocks):
        own = most[:, b * LANES : (b + 1) * LANES]
        slots[pl.ds(NEIGH * blocks + b, 1), :] = jnp.maximum(own, pltpu.roll(own, LANES - 1, 1))
    low = low_half()
    far = odd("dom")
    ghost = to_far.shape[0] // 4
    for i in range(0, ghost, 2):
        to_far[pl.ds(4 * i, 8), :] = two_rows(field, send[far, i] * 4, send[far, i + 1] * 4, low)
        to_near[pl.ds(4 * i, 8), :] = two_rows(field, send[1 - far, i] * 4, send[1 - far, i + 1] * 4, low)


def weights_body(
    send_hbm, listed, edge_angle, edge_speed, field,
    weight, base, share_weight, share_base, plane_weight, pick, slots, share_slots, order, send, sems,
):
    rows = listed.shape[0]
    copies = [
        pltpu.make_async_copy(listed.at[r], slots.at[pl.ds(r * LANES, LANES)], sems.at[r]) for r in range(rows)
    ]
    copies.append(pltpu.make_async_copy(send_hbm, send, sems.at[rows]))
    for copy in copies:
        copy.start()
    sector = 16
    nodes = edge_angle.shape[1]
    freq = 4 * LANES // sector
    first = lax.axis_index("dir") * sector
    number = lax.broadcasted_iota(jnp.int32, (sector, nodes), 0) + first
    angle = (2.0 * math.pi) * number.astype(F32) / NDIR
    parts = []
    total = jnp.ones((sector, nodes), F32)
    for j in range(NEIGH):
        part = edge_speed[pl.ds(j, 1), :] * jnp.maximum(jnp.cos(angle - edge_angle[pl.ds(j, 1), :]), 0.0)
        parts.append(part)
        total = total + part
    inverse = 1.0 / total
    spread = (
        lax.broadcasted_iota(jnp.int32, (3 * sector, 4 * LANES), 0) % sector
        == lax.broadcasted_iota(jnp.int32, (3 * sector, 4 * LANES), 1) // freq
    ).astype(F32).astype(jnp.bfloat16)

    def widened(value):
        high = value.astype(jnp.bfloat16)
        rest = value - high.astype(F32)
        middle = rest.astype(jnp.bfloat16)
        last = (rest - middle.astype(F32)).astype(jnp.bfloat16)
        pieces = jnp.concatenate([high, middle, last], axis=0)
        return lax.dot_general(pieces, spread, (((0,), (0,)), ((), ())), preferred_element_type=F32)

    ghost = send.shape[1]
    number = (lax.broadcasted_iota(jnp.int32, (2 * ghost, LANES), 0) + nodes) * 4
    blocks = nodes // LANES
    for j in range(NEIGH):
        for b in range(blocks):
            chosen = (number == listed[pl.ds(j * blocks + b, 1), :]).astype(F32).astype(jnp.bfloat16)
            pick[pl.ds(j * 6 * ghost, 6 * ghost), b * LANES : (b + 1) * LANES] = jnp.concatenate([chosen] * 3, axis=0)
        plane_weight[pl.ds(j * sector, sector), :] = parts[j] * inverse
        wide = widened(parts[j] * inverse)
        for c in range(4):
            weight[pl.ds(PAD + j * 4 * nodes + c, nodes, stride=4), :] = wide[:, c * LANES : (c + 1) * LANES]
    wide = widened(inverse)
    for c in range(4):
        rows = pl.ds(PAD + c, nodes, stride=4)
        base[rows, :] = field[rows, :] * wide[:, c * LANES : (c + 1) * LANES]
    for copy in copies:
        copy.wait()
    low = low_half()
    far = odd("dom")
    for k, row in enumerate((far, 1 - far)):
        for i in range(0, ghost, 2):
            n = send[row, i]
            m = send[row, i + 1]
            s = k * ghost + i
            share_base[pl.ds(4 * s, 8), :] = two_rows(base, n * 4, m * 4, low)
            for j in range(NEIGH):
                skip = j * 4 * nodes
                share_weight[pl.ds((j * 2 * ghost + s) * 4, 8), :] = two_rows(weight, n * 4 + skip, m * 4 + skip, low)
                share_slots[j * 2 * ghost + s] = slots[j * nodes + n]
                share_slots[j * 2 * ghost + s + 1] = slots[j * nodes + m]

    pairs = nodes // 2

    def place(i, counts):
        own, other = counts
        shared = (slots[NEIGH * nodes + 2 * i] >= 4 * nodes).astype(jnp.int32)
        order[jnp.where(shared > 0, pairs - 1 - other, own)] = i
        return own + 1 - shared, other + shared

    own, _ = lax.fori_loop(0, pairs, place, (jnp.int32(0), jnp.int32(0)), unroll=8)
    order[pairs] = own


def place_ghosts(field, from_far, from_near, nodes):
    part = lax.axis_index("dom")
    last = lax.axis_size("dom") - 1
    rows = from_far.shape[0]
    start = PAD + 4 * nodes
    far = odd("dom")
    inside = jnp.logical_and(part > 0, part < last)
    field[pl.ds(pl.multiple_of(start + far * rows, 8), rows), :] = jnp.where(inside, from_far[...], 0.0)
    field[pl.ds(pl.multiple_of(start + (1 - far) * rows, 8), rows), :] = from_near[...]


def share_rows(slots, field, weight, base, out, first):
    low = low_half()
    ghost = out.shape[0] // 4
    for i in range(0, ghost, 2):
        s = first + i
        total = base[pl.ds(4 * s, 8), :]
        for j in range(NEIGH):
            at = j * 2 * ghost + s
            total = total + weight[pl.ds(4 * at, 8), :] * two_rows(field, slots[at], slots[at + 1], low)
        out[pl.ds(4 * i, 8), :] = total


def shared_body(slots, field_in, from_far, from_near, weight, base, field, to_far, to_near):
    del field_in
    ghost = to_far.shape[0] // 4
    place_ghosts(field, from_far, from_near, (field.shape[0] - 2 * PAD) // 4 - 2 * ghost)
    share_rows(slots, field, weight, base, to_far, 0)
    share_rows(slots, field, weight, base, to_near, ghost)


def pair_row(slots, field, weight, base, i, nodes, low):
    n = i * 2
    row = pl.multiple_of(i * 8, 8)
    total = base[pl.ds(PAD + row, 8), :]
    for j in range(NEIGH):
        value = two_rows(field, slots[j * nodes + n], slots[j * nodes + n + 1], low)
        total = total + weight[pl.ds(PAD + j * 4 * nodes + row, 8), :] * value
    return row, total


def clear_ghosts(out, nodes):
    rows = out.shape[0] - 2 * PAD - 4 * nodes
    out[pl.ds(PAD + 4 * nodes, rows), :] = jnp.zeros((rows, LANES), F32)


def all_pairs(slots, field, weight, base, out, offset):
    low = low_half()
    nodes = (base.shape[0] - 2 * PAD) // 4

    def step(i, carry):
        row, total = pair_row(slots, field, weight, base, i, nodes, low)
        out[pl.ds(offset + row, 8), :] = total
        return carry

    lax.fori_loop(0, nodes // 2, step, 0, unroll=2 * GROUP)


def listed_pairs(order, slots, field, weight, base, out, first, until):
    low = low_half()
    nodes = (base.shape[0] - 2 * PAD) // 4

    def step(g, carry):
        for u in range(GROUP):
            row, total = pair_row(slots, field, weight, base, order[g * GROUP + u], nodes, low)
            out[pl.ds(PAD + row, 8), :] = total
        return carry

    lax.fori_loop(first, until, step, 0)


def early_groups(order, nodes):
    return jnp.minimum(order[nodes // 2] // GROUP, EARLY)


def first_body(order, slots, field, weight, base, swept, second):
    nodes = (base.shape[0] - 2 * PAD) // 4
    all_pairs(slots, field, weight, base, swept, PAD)
    clear_ghosts(second, nodes)
    listed_pairs(order, slots, swept, weight, base, second, 0, early_groups(order, nodes))


def second_body(order, slots, field, weight, base, second_in, second, planes, rows):
    del second_in
    nodes = (base.shape[0] - 2 * PAD) // 4
    listed_pairs(order, slots, field, weight, base, second, early_groups(order, nodes), nodes // (2 * GROUP))
    all_pairs(slots, second, weight, base, rows, 0)
    for c in range(planes.shape[0] // LANES):
        planes[pl.ds(c * LANES, LANES), :] = rows[pl.ds(c, nodes, stride=4), :].T


def received_rows(from_far, from_near, c):
    count = from_far.shape[0] // 4
    part = lax.axis_index("dom")
    inside = jnp.logical_and(part > 0, part < lax.axis_size("dom") - 1)
    far = jnp.where(inside, from_far[pl.ds(c, count, stride=4), :], 0.0)
    near = from_near[pl.ds(c, count, stride=4), :]
    swap = odd("dom") > 0
    return jnp.concatenate([jnp.where(swap, near, far), jnp.where(swap, far, near)], axis=0)


def in_pieces(value):
    high = value.astype(jnp.bfloat16)
    rest = value - high.astype(F32)
    middle = rest.astype(jnp.bfloat16)
    last = (rest - middle.astype(F32)).astype(jnp.bfloat16)
    return jnp.concatenate([high, middle, last], axis=0)


def selected(pieces, pick, j):
    depth = pieces.shape[0]
    return lax.dot_general(
        pieces, pick[pl.ds(j * depth, depth), :], (((0,), (0,)), ((), ())), preferred_element_type=F32
    )


def arrive_body(from_far, from_near, pick, plane_weight, planes, to_far, to_near):
    freq = to_far.shape[0]
    sector = planes.shape[0] // freq
    rows = received_rows(from_far, from_near, 0)
    lane = lax.broadcasted_iota(jnp.int32, rows.shape, 1)
    pieces = in_pieces(jnp.where(lane < freq, rows, received_rows(from_far, from_near, 3)))
    first = planes[pl.ds(0, freq), :]
    last = planes[pl.ds((sector - 1) * freq, freq), :]
    for j in range(NEIGH):
        found = selected(pieces, pick, j)
        first = first + plane_weight[pl.ds(j * sector, 1), :] * found[:freq, :]
        last = last + plane_weight[pl.ds(j * sector + sector - 1, 1), :] * found[LANES - freq :, :]
    far = odd("dir") > 0
    to_far[...] = jnp.where(far, last, first)
    to_near[...] = jnp.where(far, first, last)


def finished(plane, before, after, direction, rate, bearing, shift):
    angle = (2.0 * math.pi) * direction.astype(F32) / NDIR
    speed = rate * jnp.sin(angle - bearing)
    value = plane - (jnp.maximum(speed, 0.0) * (plane - before) + jnp.minimum(speed, 0.0) * (after - plane))
    freq = plane.shape[0]
    row = lax.broadcasted_iota(jnp.int32, plane.shape, 0)
    under = jnp.where(row == 0, 0.0, pltpu.roll(value, 1, 0))
    over = jnp.where(row == freq - 1, 0.0, pltpu.roll(value, freq - 1, 0))
    return value - (jnp.maximum(shift, 0.0) * (value - under) + jnp.minimum(shift, 0.0) * (over - value))


def inner_body(
    from_far, from_near, pick, plane_weight, planes, rate, bearing, shift, out, ends, swept, stage, sems
):
    freq, nodes = rate.shape
    chunks = swept.shape[0] // LANES
    width = LANES // freq
    sector = chunks * width
    first = jnp.full((1, nodes), lax.axis_index("dir") * sector, jnp.int32)
    copies = []
    done = 1
    for c in range(chunks):
        pieces = in_pieces(received_rows(from_far, from_near, c))
        total = [planes[pl.ds((c * width + k) * freq, freq), :] for k in range(width)]
        for j in range(NEIGH):
            found = selected(pieces, pick, j)
            for k in range(width):
                w = plane_weight[pl.ds(j * sector + c * width + k, 1), :]
                total[k] = total[k] + w * found[k * freq : (k + 1) * freq, :]
        for k in range(width):
            swept[pl.ds((c * width + k) * freq, freq), :] = total[k]
        until = (c + 1) * width - 1
        for d in range(done, until):
            stage[pl.ds((d - 1) * freq, freq), :] = finished(
                swept[pl.ds(d * freq, freq), :],
                swept[pl.ds((d - 1) * freq, freq), :],
                swept[pl.ds((d + 1) * freq, freq), :],
                first + d,
                rate[...],
                bearing[...],
                shift[...],
            )
        copy = pltpu.make_async_copy(
            stage.at[pl.ds((done - 1) * freq, (until - done) * freq), :],
            out.at[pl.ds(done * freq, (until - done) * freq), :],
            sems.at[c],
        )
        copy.start()
        copies.append(copy)
        done = until
    for k, d in enumerate((0, 1, sector - 2, sector - 1)):
        ends[k] = swept[pl.ds(d * freq, freq), :]
    for copy in copies:
        copy.wait()


def edge_body(ends, from_far, from_near, rate, bearing, shift, out_in, out, stage, sem):
    del out_in
    far = odd("dir") > 0
    freq, nodes = rate.shape
    sector = out.shape[0] // freq
    first = jnp.full((1, nodes), lax.axis_index("dir") * sector, jnp.int32)
    before = jnp.where(far, from_near[...], from_far[...])
    after = jnp.where(far, from_far[...], from_near[...])
    copies = []
    for k, (d, low, plane, high) in enumerate(
        ((0, before, ends[0], ends[1]), (sector - 1, ends[2], ends[3], after))
    ):
        stage[k] = finished(plane, low, high, first + d, rate[...], bearing[...], shift[...])
        copy = pltpu.make_async_copy(stage.at[k], out.at[pl.ds(d * freq, freq), :], sem.at[k])
        copy.start()
        copies.append(copy)
    for copy in copies:
        copy.wait()


def swap_far_parts(array):
    count, width = (lax.axis_size("dom"), lax.axis_size("dir"))
    pairs = []
    for d in range(width):
        for i in range(1, count - 1, 2):
            here, there = (i * width + d, (i + 1) * width + d)
            pairs += [(here, there), (there, here)]
        for i in (0, count - 1):
            pairs.append((i * width + d, i * width + (d ^ 1)))
    return lax.ppermute(array, ("dom", "dir"), pairs)


def swap_far_sectors(array):
    count = lax.axis_size("dir")
    pairs = [p for i in range(1, count, 2) for p in ((i, (i + 1) % count), ((i + 1) % count, i))]
    return lax.ppermute(array, "dir", pairs)


def swap_near(array, axis):
    count = lax.axis_size(axis)
    return lax.ppermute(array, axis, [p for i in range(0, count, 2) for p in ((i, i + 1), (i + 1, i))])


def shards(
    action, edge_angle, edge_speed, neighbours, send_rows, refract_rate, refract_angle, shift_rate
):
    sector, freq, nodes = action.shape
    ghost = send_rows.shape[1]
    field_rows = 4 * (nodes + 2 * ghost) + 2 * PAD
    fields = jax.ShapeDtypeStruct((field_rows, LANES), F32)
    shares = jax.ShapeDtypeStruct((4 * ghost, LANES), F32)
    weights = jax.ShapeDtypeStruct((NEIGH * 4 * nodes + 2 * PAD, LANES), F32)
    bases = jax.ShapeDtypeStruct((4 * nodes + 2 * PAD, LANES), F32)
    columns = sector * freq
    bearing = refract_angle.reshape(1, nodes)

    edges = jax.ShapeDtypeStruct((NEIGH, nodes), F32)
    field, far, near, angle, speed, slots = pl.pallas_call(
        rows_body,
        out_shape=(fields, shares, shares, edges, edges, jax.ShapeDtypeStruct(((NEIGH + 2) * nodes // LANES, LANES), jnp.int32)),
        in_specs=[HBM] * 5,
        out_specs=(VMEM,) * 6,
        scratch_shapes=[
            pltpu.VMEM((columns // LANES, LANES, nodes), F32),
            pltpu.SMEM((2, ghost), jnp.int32),
            pltpu.VMEM((NEIGH, nodes), jnp.int32),
            pltpu.SemaphoreType.DMA((columns // LANES + 4,)),
        ],
        compiler_params=params(),
        name="rows",
    )(*(in_hbm(x) for x in (send_rows, action.reshape(columns, nodes), edge_angle, edge_speed, neighbours)))
    far = swap_far_parts(far)
    near = swap_near(near, "dom")
    weight, base, share_weight, share_base, plane_weight, pick, slots, share_slots, order = pl.pallas_call(
        weights_body,
        out_shape=(
            weights,
            bases,
            jax.ShapeDtypeStruct((NEIGH * 8 * ghost, LANES), F32),
            jax.ShapeDtypeStruct((8 * ghost, LANES), F32),
            jax.ShapeDtypeStruct((NEIGH * sector, nodes), F32),
            jax.ShapeDtypeStruct((NEIGH * 6 * ghost, nodes), jnp.bfloat16),
            pltpu.SMEM(((NEIGH + 2) * nodes,), jnp.int32),
            pltpu.SMEM((NEIGH * 2 * ghost,), jnp.int32),
            pltpu.SMEM((nodes // 2 + 8,), jnp.int32),
        ),
        in_specs=[HBM] + [VMEM] * 4,
        out_specs=(VMEM,) * 6 + (SMEM,) * 3,
        scratch_shapes=[
            pltpu.SMEM((2, ghost), jnp.int32),
            pltpu.SemaphoreType.DMA(((NEIGH + 2) * nodes // LANES + 1,)),
        ],
        compiler_params=params(),
        cost_estimate=cost(1 << 30, 8 << 20),
        name="weights",
    )(in_hbm(send_rows), slots, angle, speed, field)

    def shared(field, far, near):
        field, far, near = pl.pallas_call(
            shared_body,
            out_shape=(fields, shares, shares),
            in_specs=[SMEM] + [VMEM] * 5,
            out_specs=(VMEM, VMEM, VMEM),
            input_output_aliases={1: 0},
            compiler_params=params(),
            name="shared",
        )(share_slots, field, far, near, share_weight, share_base)
        return field, swap_far_parts(far), swap_near(near, "dom")

    field, far, near = shared(field, far, near)
    field, second = pl.pallas_call(
        first_body,
        out_shape=(fields, fields),
        in_specs=[SMEM, SMEM] + [VMEM] * 3,
        out_specs=(VMEM, VMEM),
        compiler_params=params(),
        cost_estimate=cost(1 << 30, 8 << 20),
        name="first_sweep",
    )(order, slots, field, weight, base)
    field, far, near = shared(field, far, near)
    _, planes = pl.pallas_call(
        second_body,
        out_shape=(fields, jax.ShapeDtypeStruct((columns, nodes), F32)),
        in_specs=[SMEM, SMEM] + [VMEM] * 4,
        out_specs=(VMEM, VMEM),
        input_output_aliases={5: 0},
        scratch_shapes=[pltpu.VMEM((4 * nodes, LANES), F32)],
        compiler_params=params(),
        cost_estimate=cost(1 << 31, 16 << 20),
        name="second_sweep",
    )(order, slots, field, weight, base, second)

    edge = jax.ShapeDtypeStruct((freq, nodes), F32)
    plane_shape = jax.ShapeDtypeStruct((columns, nodes), F32)
    far_plane, near_plane = pl.pallas_call(
        arrive_body,
        out_shape=(edge, edge),
        in_specs=[VMEM] * 5,
        out_specs=(VMEM, VMEM),
        compiler_params=params(),
        name="last_sweep_edges",
    )(far, near, pick, plane_weight, planes)
    far_plane = swap_far_sectors(far_plane)
    near_plane = swap_near(near_plane, "dir")
    out, ends = pl.pallas_call(
        inner_body,
        out_shape=(plane_shape, jax.ShapeDtypeStruct((4, freq, nodes), F32)),
        in_specs=[VMEM] * 8,
        out_specs=(ANY, VMEM),
        scratch_shapes=[
            pltpu.VMEM((columns, nodes), F32),
            pltpu.VMEM((columns - 2 * freq, nodes), F32),
            pltpu.SemaphoreType.DMA((4,)),
        ],
        compiler_params=params(),
        cost_estimate=cost(1 << 28, 2 << 20),
        name="inner_planes",
    )(far, near, pick, plane_weight, planes, refract_rate, bearing, shift_rate)
    out = pl.pallas_call(
        edge_body,
        out_shape=plane_shape,
        in_specs=[VMEM] * 6 + [ANY],
        out_specs=ANY,
        input_output_aliases={6: 0},
        scratch_shapes=[pltpu.VMEM((2, freq, nodes), F32), pltpu.SemaphoreType.DMA((2,))],
        compiler_params=params(),
        name="edge_planes",
    )(ends, far_plane, near_plane, refract_rate, bearing, shift_rate, out)
    return out.reshape(sector, freq, nodes)


def solution(mesh):
    return jax.shard_map(
        shards,
        mesh=mesh,
        in_specs=(
            P("dir", None, "dom"),
            P(None, "dom"),
            P(None, "dom"),
            P(None, "dom"),
            P(None, "dom"),
            P(None, "dom"),
            P("dom"),
            P(None, "dom"),
        ),
        out_specs=P("dir", None, "dom"),
        check_vma=False,
    )
```
